128 devices in a mesh: curve: 128 (over y, x, z, core).
Axes of the slice: x: 4, y: 4, z: 4, core: 2. Of those that a mesh axis runs over, the one named last changes fastest.
Arguments:
- diag_blocks: bfloat16 [8192, 128, 128], P('curve'), may hold values from 0.049804688 to 1
- super_blocks: bfloat16 [8192, 4, 128, 128], P('curve'), may hold values from 0.049804688 to 1
- far_blocks: bfloat16 [32768, 128, 128], P('curve'), may hold values from 0.049804688 to 1
- far_row: int32 [32768], P('curve'), may hold values from -1 to 63, as said below
- send_slot: int32 [32768], P('curve'), may hold values from -1 to 63, as said below
- start_panel: float32 [64, 1048576], P(None, 'curve'), may hold values from -6 to 6
Outputs:
- basis: float32 [64, 1048576], P(None, 'curve')
- update: float32 [64, 1048576], P(None, 'curve')
The draws below stay inside these ranges and needn't reach their ends.
Inputs may be any that keep to these rules, and one draw needn't show every extreme that they name: `send_slot`: at most 2 live slots from one owner to one reader; some owner fills all 2 slots to every reader. `far_row`: empty slots match those of send_slot.
All inputs are finite; a program needn't handle non-finite values.
Results may differ from the reference program's by a relative error of at most 0.0026.
Values may be sent and summed in bfloat16 or wider, within the bound.
A program may use at most 256 MiB of HBM per device.

```python
import jax
import jax.numpy as jnp
from jax import lax

K = 64
BS = 128
HB = 4
RB = 64
FAR = 256
ITERS = 2
CAP = 2
BLOCKS = 8192
POINTS = 1048576
SLOTS = 32768
N_CURVE = 128


def slot_tables(key):
    base = jax.random.fold_in(key, 17)
    keys = jax.random.split(base, 5)
    owners = FAR // CAP
    hubs = jax.random.randint(keys[0], (owners,), 0, 4) == 0
    forced = jax.random.randint(keys[1], (), 0, owners)
    hubs = hubs | (jnp.arange(owners) == forced)
    lighter = jax.random.randint(keys[2], (owners, owners), 0, CAP // 2 + 1)
    loads = jnp.where(hubs[:, None], CAP, lighter)
    live = jnp.arange(CAP)[None, None, :] < loads[:, :, None]
    slots = jax.random.randint(keys[3], (owners, owners, CAP), 0, RB)
    rows = jax.random.randint(keys[4], (owners, owners, CAP), 0, RB)
    return (jnp.where(live, slots, -1).astype(jnp.int32), jnp.where(live, rows, -1).astype(jnp.int32))


def draw_send_slot(key, part):
    slots, rows = slot_tables(key)
    return slots.reshape(-1)


def draw_far_row(key, part):
    slots, rows = slot_tables(key)
    return rows.transpose(1, 0, 2).reshape(-1)


def levels(stream_key, shape, cuts, low, high):
    def one(axis_at, shards_of):
        heights = jax.random.uniform(jax.random.fold_in(jax.random.fold_in(stream_key, 6), axis_at), (shards_of,), jnp.float32, low / len(cuts), high / len(cuts))
        return jnp.repeat(jnp.exp(heights), shape[axis_at] // shards_of).reshape((-1,) + (1,) * (len(shape) - axis_at - 1))

    factor_of = one(*cuts[0])
    for cut in cuts[1:]:
        factor_of = factor_of * one(*cut)
    return factor_of


def normal_values(rng, extent, width, reach, shards=(), kind=jnp.bfloat16):
    level = levels(rng, extent, shards, -0.22, 0.18) if shards else 1.0
    values = jax.random.normal(rng, extent, jnp.float32) * width * level
    return jnp.minimum(jnp.maximum(values, -reach), reach).astype(kind)


def setup_inputs(seed: int = 0) -> dict:
    key_list = jax.random.split(jax.random.key(seed), 7)
    return {
        "diag_blocks": jnp.clip(0.049804688 + 0.9501953 * jax.random.uniform(key_list[0], (BLOCKS, BS, BS), jnp.float32) ** levels(key_list[0], (BLOCKS, BS, BS), ((0, 128),), -0.2, 0.2), 0.049804688, 1.0).astype(jnp.bfloat16),
        "super_blocks": jnp.clip(0.049804688 + 0.9501953 * jax.random.uniform(key_list[1], (BLOCKS, HB, BS, BS), jnp.float32) ** levels(key_list[1], (BLOCKS, HB, BS, BS), ((0, 128),), -0.2, 0.2), 0.049804688, 1.0).astype(jnp.bfloat16),
        "far_blocks": jnp.clip(0.049804688 + 0.9501953 * jax.random.uniform(key_list[2], (SLOTS, BS, BS), jnp.float32) ** levels(key_list[2], (SLOTS, BS, BS), ((0, 128),), -0.2, 0.2), 0.049804688, 1.0).astype(jnp.bfloat16),
        "far_row": draw_far_row(jax.random.fold_in(key_list[6], 71), 0),
        "send_slot": draw_send_slot(jax.random.fold_in(key_list[6], 71), 0),
        "start_panel": normal_values(key_list[5], (K, POINTS), 1.0, 6.0, ((1, 128),), jnp.float32),
    }


exact_mode = lax.Precision.HIGHEST
step_size = 10.0
momentum = 0.5

def to_blocks(matrix):
    return matrix.reshape(matrix.shape[0], BLOCKS, BS).transpose(1, 0, 2)

def from_blocks(blocks):
    return blocks.transpose(1, 0, 2).reshape(blocks.shape[1], POINTS)

def apply_w(panel, diag_blocks, super_blocks, far_blocks, far_row, send_slot):
    vals = panel.astype(jnp.float32)
    diag_f = diag_blocks.astype(jnp.float32)
    result = jnp.einsum('bcp,bqp->bcq', vals, diag_f, precision=exact_mode)
    result = result + jnp.einsum('bcp,bpq->bcq', vals, diag_f, precision=exact_mode)
    for band in range(HB):
        upper = super_blocks[:, band].astype(jnp.float32)
        result = result + jnp.einsum('bcp,bqp->bcq', jnp.roll(vals, -(band + 1), axis=0), upper, precision=exact_mode)
        lower_terms = jnp.einsum('bcp,bpq->bcq', vals, upper, precision=exact_mode)
        result = result + jnp.roll(lower_terms, band + 1, axis=0)
    owners = N_CURVE
    slot_table = send_slot.reshape(owners, owners, CAP).transpose(1, 0, 2).reshape(owners, FAR)
    owner_base = (jnp.repeat(jnp.arange(owners, dtype=jnp.int32), CAP) * RB).astype(jnp.int32)
    row_table = far_row.reshape(owners, FAR)
    block_table = far_blocks.reshape(owners, FAR, BS, BS)

    def reader_step(carry, items):
        reader, rows, slots, blocks = items
        live = ((rows >= 0) & (slots >= 0))[:, None, None]
        grow = (reader * RB + jnp.maximum(rows, 0)).astype(jnp.int32)
        gcol = (owner_base + jnp.maximum(slots, 0)).astype(jnp.int32)
        blocks_f = blocks.astype(jnp.float32)
        forward = jnp.einsum('fcp,fqp->fcq', vals[gcol], blocks_f, precision=exact_mode)
        mirror = jnp.einsum('fcp,fpq->fcq', vals[grow], blocks_f, precision=exact_mode)
        carry = carry.at[grow].add(jnp.where(live, forward, 0.0))
        carry = carry.at[gcol].add(jnp.where(live, mirror, 0.0))
        return (carry, None)
    readers = jnp.arange(owners, dtype=jnp.int32)
    result, _ = lax.scan(reader_step, result, (readers, row_table, slot_table, block_table))
    return result

def lower_inverse(cross):
    factor = jnp.linalg.cholesky(cross)
    return lax.linalg.triangular_solve(factor, jnp.eye(cross.shape[0], dtype=cross.dtype), left_side=True, lower=True)

def reference(diag_blocks, super_blocks, far_blocks, far_row, send_slot, start_panel):
    unit_panel = jnp.ones((BLOCKS, 1, BS), jnp.bfloat16)
    degree = from_blocks(apply_w(unit_panel, diag_blocks, super_blocks, far_blocks, far_row, send_slot))
    inv_root = lax.rsqrt(degree)
    start_gram = jnp.dot(start_panel, start_panel.T, precision=exact_mode) / POINTS
    current = jnp.dot(lower_inverse(start_gram), start_panel, precision=exact_mode)
    change = jnp.zeros_like(current)
    for step in range(ITERS):
        scaled = (inv_root * current).astype(jnp.bfloat16)
        image = inv_root * from_blocks(apply_w(to_blocks(scaled), diag_blocks, super_blocks, far_blocks, far_row, send_slot))
        rayleigh = jnp.dot(current, image.T, precision=exact_mode) / POINTS
        resid = image - jnp.dot(rayleigh.T, current, precision=exact_mode)
        trial = current + step_size * resid + momentum * change
        cross = jnp.dot(trial, trial.T, precision=exact_mode) / POINTS
        fresh = jnp.dot(lower_inverse(cross), trial, precision=exact_mode)
        change = fresh - current
        current = fresh
    return (current, change)
```

```python
import functools

import jax
import jax.numpy as jnp
from jax import lax
from jax.experimental import pallas as pl
from jax.experimental.pallas import tpu as pltpu
from jax.sharding import PartitionSpec as P

f32, bf16, i32 = jnp.float32, jnp.bfloat16, jnp.int32
HIGH = lax.Precision.HIGHEST
STEP = 10.0
MOMENTUM = 0.5
MESH = pl.DeviceIdType.MESH
VMEM = pltpu.VMEM
DMA = pltpu.SemaphoreType.DMA
VM_LIMIT = 60 * 2**20


def nn(a, b, precision=None):
    return lax.dot_general(a, b, (((1,), (0,)), ((), ())), precision=precision, preferred_element_type=f32)


def nt(a, b, precision=None):
    return lax.dot_general(a, b, (((1,), (1,)), ((), ())), precision=precision, preferred_element_type=f32)


def halves(x):
    hi = x.astype(bf16)
    return hi, (x - hi.astype(f32)).astype(bf16)


def nn3(a, b):
    (ah, al), (bh, bl) = halves(a), halves(b)
    return nn(ah, bh) + (nn(ah, bl) + nn(al, bh))


def nt3(a, b):
    (ah, al), (bh, bl) = halves(a), halves(b)
    return nt(ah, bh) + (nt(ah, bl) + nt(al, bh))


def eye(n, m=None):
    m = m or n
    rows = lax.broadcasted_iota(i32, (n, m), 0)
    return (rows == lax.broadcasted_iota(i32, (n, m), 1)).astype(f32)


def chol_inverse(cross):
    n = cross.shape[0]
    both = jnp.concatenate([cross, eye(n)], axis=1)
    tiles = [both[8 * i : 8 * i + 8] for i in range(n // 8)]
    row_id = lax.broadcasted_iota(i32, (8, 1), 0)
    for k in range(n):
        at, sub = k // 8, k % 8
        row = tiles[at][sub : sub + 1]
        row = row / row[:, k : k + 1]
        for i in range(at, n // 8):
            column = tiles[i][:, k : k + 1]
            if i == at:
                column = jnp.where(row_id > sub, column, 0.0)
            tiles[i] = tiles[i] - column * row
    both = jnp.concatenate(tiles, axis=0)
    pivots = jnp.sum(both[:, :n] * eye(n), axis=1, keepdims=True)
    return both[:, n:] * lax.rsqrt(pivots)


def position():
    me = lax.axis_index("curve")
    return me, me // 32, (me // 8) % 4, (me // 2) % 4, me % 2


def partner(k):
    me, y, x, z, c = position()
    dz = (k // 2) % 4
    y, x, z, c = (y + k // 32 + dz) % 4, (x + k // 8 + dz) % 4, (z + dz) % 4, (c + k) % 2
    return ((y * 4 + x) * 4 + z) * 2 + c


def greet_all(n):
    barrier = pltpu.get_barrier_semaphore()

    @pl.loop(1, n)
    def _(k):
        pl.semaphore_signal(barrier, inc=1, device_id=(partner(k),), device_id_type=MESH)

    pl.semaphore_wait(barrier, n - 1)


def send(src, dst, ssem, rsem, to):
    copy = pltpu.make_async_remote_copy(
        src_ref=src, dst_ref=dst, send_sem=ssem, recv_sem=rsem, device_id=(to,), device_id_type=MESH
    )
    copy.start()
    return copy


def drain(ref, sem):
    pltpu.make_async_copy(ref, ref, sem).wait()


class Reduction:
    @staticmethod
    def scratch(rows):
        piece = rows // 8
        return [
            VMEM((8, piece, 128), f32),
            VMEM((8, piece, 128), f32),
            VMEM((4, piece, 128), f32),
            VMEM((4, piece, 128), f32),
            VMEM((8, piece, 128), f32),
            DMA((4,)),
            DMA((4,)),
        ]

    def __init__(self, refs):
        self.src, self.first, self.second, self.third, self.out, self.ss, self.rs = refs
        me, self.y, self.x, _, _ = position()
        self.sub = me % 8
        self.base = me - self.sub

    def peers(self):
        near = [self.base + (self.sub + k) % 8 for k in range(1, 8)]
        across = [((self.y * 4 + (self.x + k) % 4) * 8 + self.sub) for k in range(1, 4)]
        up = [(((self.y + k) % 4 * 4 + self.x) * 8 + self.sub) for k in range(1, 4)]
        return near, across, up

    def start(self, value):
        piece = value.shape[0] // 8
        for i in range(8):
            self.src[i] = value[i * piece : (i + 1) * piece]
        for k in range(1, 8):
            other = (self.sub + k) % 8
            send(self.src.at[other], self.first.at[self.sub], self.ss.at[0], self.rs.at[0], self.base + other)
        self.first[self.sub] = self.src[self.sub]

    def across(self):
        drain(self.first.at[pl.ds(0, 7)], self.rs.at[0])
        total = self.first[0]
        for i in range(1, 8):
            total = total + self.first[i]
        self.second[self.x] = total
        for k in range(1, 4):
            to = (self.y * 4 + (self.x + k) % 4) * 8 + self.sub
            send(self.second.at[self.x], self.second.at[self.x], self.ss.at[1], self.rs.at[1], to)

    def up(self):
        drain(self.second.at[pl.ds(0, 3)], self.rs.at[1])
        self.third[self.y] = (self.second[0] + self.second[1]) + (self.second[2] + self.second[3])
        for k in range(1, 4):
            to = ((self.y + k) % 4 * 4 + self.x) * 8 + self.sub
            send(self.third.at[self.y], self.third.at[self.y], self.ss.at[2], self.rs.at[2], to)

    def gather(self):
        drain(self.third.at[pl.ds(0, 3)], self.rs.at[2])
        self.out[self.sub] = (self.third[0] + self.third[1]) + (self.third[2] + self.third[3])
        for k in range(1, 8):
            send(
                self.out.at[self.sub],
                self.out.at[self.sub],
                self.ss.at[3],
                self.rs.at[3],
                self.base + (self.sub + k) % 8,
            )

    def result(self):
        drain(self.out.at[pl.ds(0, 7)], self.rs.at[3])
        drain(self.src.at[pl.ds(0, 7)], self.ss.at[0])
        drain(self.second.at[pl.ds(0, 3)], self.ss.at[1])
        drain(self.third.at[pl.ds(0, 3)], self.ss.at[2])
        drain(self.out.at[pl.ds(0, 7)], self.ss.at[3])
        return jnp.concatenate([self.out[i] for i in range(8)], axis=0)


def block(b):
    return pl.ds(pl.multiple_of(b * 128, 128), 128)


def start_kernel(
    n, rb, bands, points,
    far_row, send_slot, panel, diag_hbm, super_hbm, far_hbm,
    x_out, v_out, root_out,
    diag, sup, far, deg, far_sums, cols, cols_in, tail_in, load_sem, small_sem,
    *reduction,
):
    width = panel.shape[0]
    slots = far.shape[0]
    loads = [
        pltpu.make_async_copy(diag_hbm, diag, load_sem.at[0]),
        pltpu.make_async_copy(super_hbm, sup, load_sem.at[1]),
        pltpu.make_async_copy(far_hbm, far, load_sem.at[2]),
    ]
    for load in loads:
        load.start()
    greet_all(n)
    total = Reduction(reduction)
    me = lax.axis_index("curve")

    hi, lo = halves(panel[...])
    cross = nt(hi, lo)
    gram = nt(hi, hi) + (cross + cross.T)
    total.start(jnp.concatenate([gram, jnp.zeros_like(gram)], axis=1))

    deg[...] = jnp.zeros_like(deg)
    ones = jnp.ones((16, 128), bf16)
    for load in loads[:2]:
        load.wait()

    def near(b, carry):
        rows = nt(ones, diag[b])[0:1] + nn(ones, diag[b])[0:1]
        for h in range(bands):
            rows = rows + nt(ones, sup[b, h])[0:1]
            deg[pl.ds(b + h + 1, 1), :] += nn(ones, sup[b, h])[0:1]
        deg[pl.ds(b, 1), :] += rows
        return carry

    lax.fori_loop(0, rb // 2, near, 0)
    total.across()
    lax.fori_loop(rb // 2, rb, near, 0)
    total.up()
    following = (me + 1) % n
    tail = send(deg.at[pl.ds(rb, 8)], tail_in, small_sem.at[0], small_sem.at[1], following)
    loads[2].wait()
    sub = lax.broadcasted_iota(i32, (8, 128), 0)

    def far_one(k, carry):
        t = partner(k)
        pair = []
        for c in range(2):
            f = 2 * t + c
            far_sums[pl.ds(f, 1), :] = nt(ones, far[f])[0:1]
            pair.append(nn(ones, far[f])[0:1])
        cols[t] = jnp.where(sub == 0, pair[0], jnp.where(sub == 1, pair[1], 0.0))
        return carry

    far_one(0, 0)
    cols_in[me] = cols[me]

    def far_step(k, carry):
        far_one(k, carry)
        t = partner(k)
        send(cols.at[t], cols_in.at[me], small_sem.at[2], small_sem.at[3], t)
        return carry

    lax.fori_loop(1, n // 2, far_step, 0)
    total.gather()
    lax.fori_loop(n // 2, n, far_step, 0)

    inverse = chol_inverse(total.result()[:, :width] * (1.0 / points))
    x0 = nn3(inverse, panel[...])
    x_out[...] = x0

    owner_rows = lax.broadcasted_iota(i32, (rb, slots), 0)
    degree = deg[0:rb, :] + nn((owner_rows == far_row[...]).astype(f32), far_sums[...], HIGH)
    tail.wait_recv()
    degree = degree + jnp.concatenate([tail_in[...], jnp.zeros((rb - 8, 128), f32)], axis=0)
    drain(cols_in.at[pl.ds(0, n - 1)], small_sem.at[3])
    slot_rows = lax.broadcasted_iota(i32, (rb, 8 * n), 0)
    degree = degree + nn((slot_rows == send_slot[...]).astype(f32), cols_in[...].reshape(8 * n, 128), HIGH)
    root = lax.rsqrt(degree)
    root_out[...] = root
    for b in range(rb):
        lanes = slice(b * 128, b * 128 + 128)
        v_out[b] = (x0[:, lanes] * root[b : b + 1]).astype(bf16)
    tail.wait_send()
    drain(cols.at[pl.ds(0, n - 1)], small_sem.at[2])


def start(n, diag_blocks, super_blocks, far_blocks, far_row, send_slot, panel):
    rb, bs = diag_blocks.shape[:2]
    bands, slots, width = super_blocks.shape[1], far_blocks.shape[0], panel.shape[0]
    owned = rb * bs
    send_pad = jnp.pad(send_slot.reshape(n, 2), ((0, 0), (0, 6)), constant_values=-1).reshape(1, 8 * n)
    here = pl.BlockSpec(memory_space=pltpu.VMEM)
    away = pl.BlockSpec(memory_space=pl.ANY)
    return pl.pallas_call(
        functools.partial(start_kernel, n, rb, bands, float(n * owned)),
        out_shape=(
            jax.ShapeDtypeStruct((width, owned), f32),
            jax.ShapeDtypeStruct((rb, width, bs), bf16),
            jax.ShapeDtypeStruct((rb, bs), f32),
        ),
        in_specs=[here, here, here, away, away, away],
        out_specs=(here, here, here),
        scratch_shapes=[
            VMEM(diag_blocks.shape, bf16),
            VMEM(super_blocks.shape, bf16),
            VMEM(far_blocks.shape, bf16),
            VMEM((rb + 8, bs), f32),
            VMEM((slots, bs), f32),
            VMEM((n, 8, bs), f32),
            VMEM((n, 8, bs), f32),
            VMEM((8, bs), f32),
            DMA((3,)),
            DMA((4,)),
            *Reduction.scratch(width),
        ],
        compiler_params=pltpu.CompilerParams(collective_id=1, has_side_effects=True, vmem_limit_bytes=VM_LIMIT),
        name="start",
    )(far_row.reshape(1, slots), send_pad, panel, diag_blocks, super_blocks, far_blocks)


def exchange_kernel(
    n, rb, bands, last,
    index, keep, v, root, diag_hbm, super_hbm, far_hbm, *rest,
):
    if last:
        x_hbm, prev_hbm, t_out, gram_out, *rest = rest
    else:
        t_out, u_out, *rest = rest
    diag, sup, far, ahead, near, stage, mirror, came, back, seg, tail_in, load_sem, sems, *rest = rest
    width, owned = v.shape[1], rb * 128
    slots = far.shape[0]
    me = lax.axis_index("curve")
    loads = [
        pltpu.make_async_copy(far_hbm, far, load_sem.at[0]),
        pltpu.make_async_copy(diag_hbm, diag, load_sem.at[1]),
        pltpu.make_async_copy(super_hbm, sup, load_sem.at[2]),
    ]
    if last:
        x0, prev = rest
        loads += [
            pltpu.make_async_copy(x_hbm, x0, load_sem.at[3]),
            pltpu.make_async_copy(prev_hbm, prev, load_sem.at[4]),
        ]
    for load in loads:
        load.start()
    greet_all(n)
    halo = send(
        v.at[pl.ds(0, bands)], ahead, sems.at[0], sems.at[1], (me + n - 1) % n
    )

    def stage_one(k):
        t = partner(k)
        for c in range(2):
            stage[2 * t + c] = v[index[0, 2 * t + c]]
        return t

    stage_one(0)
    came[pl.ds(2 * me, 2)] = stage[pl.ds(2 * me, 2)]

    def stage_step(k, carry):
        t = stage_one(k)
        send(stage.at[pl.ds(2 * t, 2)], came.at[pl.ds(2 * me, 2)], sems.at[2], sems.at[3], t)
        return carry

    lax.fori_loop(1, n, stage_step, 0)
    loads[0].wait()

    def mirror_one(k):
        t = partner(k)
        for c in range(2):
            f = 2 * t + c
            mirror[f] = nn(v[index[1, f]], far[f]).astype(bf16)
        return t

    mirror_one(0)
    back[pl.ds(2 * me, 2)] = mirror[pl.ds(2 * me, 2)]

    def mirror_step(k, carry):
        t = mirror_one(k)
        send(mirror.at[pl.ds(2 * t, 2)], back.at[pl.ds(2 * me, 2)], sems.at[4], sems.at[5], t)
        return carry

    lax.fori_loop(1, n, mirror_step, 0)

    near[...] = jnp.zeros_like(near)
    loads[1].wait()
    loads[2].wait()

    def near_one(b, fetch):
        vb = v[b]
        out = nt(vb, diag[b]) + nn(vb, diag[b])
        for h in range(bands):
            out = out + nt(fetch(b, h), sup[b, h])
            near[:, block(b + h + 1)] += nn(vb, sup[b, h])
        near[:, block(b)] += out

    def near_step(b, carry):
        near_one(b, lambda b, h: v[b + h + 1])
        return carry

    lax.fori_loop(0, rb - bands, near_step, 0)
    halo.wait_recv()
    for b in range(rb - bands, rb):

        def fetch(b, h):
            at = b + h + 1
            return v[at] if at < rb else ahead[at - rb]

        near_one(b, fetch)
    tail = send(
        near.at[:, pl.ds(owned, bands * 128)], tail_in, sems.at[6], sems.at[7], (me + 1) % n
    )
    if last:
        for load in loads[3:]:
            load.wait()
        (xh, xl), (ph, pl_) = halves(x0[...]), halves(prev[...])
        gram_out[0:width, 0:width] = nt(xh, ph) + (nt(xh, pl_) + nt(xl, ph))
        cross = nt(ph, pl_)
        gram_out[0:width, width : 2 * width] = nt(ph, ph) + (cross + cross.T)
        cross = nt(xh, xl)
        gram_out[2 * width : 3 * width, width : 2 * width] = nt(xh, xh) + (cross + cross.T)

    drain(came.at[pl.ds(0, slots - 2)], sems.at[3])
    zero = jnp.zeros((width, 128), f32)

    def forward(j4, total):
        for i in range(4):
            j = j4 * 4 + i
            f = index[2, j]
            total = total * keep[0, j] + nt(came[f], far[f])
            seg[j] = total
        return total

    lax.fori_loop(0, slots // 4, forward, zero)

    def add_forward(b, carry):
        near[:, block(b)] += seg[index[4, b]] * keep[2, b]
        return carry

    lax.fori_loop(0, rb, add_forward, 0)
    tail.wait_recv()
    near[:, 0 : bands * 128] += tail_in[...]

    drain(back.at[pl.ds(0, slots - 2)], sems.at[5])

    def backward(j4, total):
        for i in range(4):
            j = j4 * 4 + i
            total = total * keep[1, j] + back[index[3, j]].astype(f32)
            seg[j] = total
        return total

    lax.fori_loop(0, slots // 4, backward, zero)

    def finish(b, carry):
        d = root[pl.ds(b, 1), :]
        t = (near[:, block(b)] + seg[index[5, b]] * keep[3, b]) * d
        t_out[:, block(b)] = t
        if not last:
            u_out[b] = (t * d).astype(bf16)
        return carry

    lax.fori_loop(0, rb, finish, 0)
    if last:
        th, tl = halves(t_out[...])
        gram_out[width : 2 * width, 0:width] = nt(xh, th) + (nt(xh, tl) + nt(xl, th))
        gram_out[width : 2 * width, width : 2 * width] = nt(ph, th) + (nt(ph, tl) + nt(pl_, th))
        cross = nt(th, tl)
        gram_out[2 * width : 3 * width, 0:width] = nt(th, th) + (cross + cross.T)
    halo.wait_send()
    tail.wait_send()
    drain(stage.at[pl.ds(0, slots - 2)], sems.at[2])
    drain(mirror.at[pl.ds(0, slots - 2)], sems.at[4])


def exchange(n, tables, v, root, diag_blocks, super_blocks, far_blocks, extra):
    rb, bs = diag_blocks.shape[:2]
    bands, slots = super_blocks.shape[1], far_blocks.shape[0]
    width, owned = v.shape[1], rb * bs
    last = bool(extra)
    here = pl.BlockSpec(memory_space=pltpu.VMEM)
    away = pl.BlockSpec(memory_space=pl.ANY)
    scalar = pl.BlockSpec(memory_space=pltpu.SMEM)
    outs = [jax.ShapeDtypeStruct((width, owned), f32)]
    outs.append(
        jax.ShapeDtypeStruct((3 * width, 2 * width), f32) if last else jax.ShapeDtypeStruct((rb, width, bs), bf16)
    )
    return pl.pallas_call(
        functools.partial(exchange_kernel, n, rb, bands, last),
        out_shape=tuple(outs),
        in_specs=[scalar, scalar, here, here, away, away, away] + [away] * len(extra),
        out_specs=(here, here),
        scratch_shapes=[
            VMEM(diag_blocks.shape, bf16),
            VMEM(super_blocks.shape, bf16),
            VMEM(far_blocks.shape, bf16),
            VMEM((bands, width, bs), bf16),
            VMEM((width, owned + bands * bs), f32),
            VMEM((slots, width, bs), bf16),
            VMEM((slots, width, bs), bf16),
            VMEM((slots, width, bs), bf16),
            VMEM((slots, width, bs), bf16),
            VMEM((slots, width, bs), f32),
            VMEM((width, bands * bs), f32),
            DMA((3 + len(extra),)),
            DMA((8,)),
            *[VMEM((width, owned), f32) for _ in extra],
        ],
        compiler_params=pltpu.CompilerParams(
            collective_id=3 if last else 2, has_side_effects=True, vmem_limit_bytes=VM_LIMIT
        ),
        name="last_exchange" if last else "first_exchange",
    )(*tables, v, root, diag_blocks, super_blocks, far_blocks, *extra)


def small_kernel(points, gram, coef, *reduction):
    barrier = pltpu.get_barrier_semaphore()
    total = Reduction(reduction)
    near, across, up = total.peers()
    for to in near + across + up:
        pl.semaphore_signal(barrier, inc=1, device_id=(to,), device_id_type=MESH)
    pl.semaphore_wait(barrier, 13)
    total.start(gram[...])
    total.across()
    total.up()
    total.gather()
    w = gram.shape[1] // 2
    sums = total.result() * (1.0 / points)
    h01, h11 = sums[0:w, 0:w], sums[0:w, w:]
    h02, h12 = sums[w : 2 * w, 0:w], sums[w : 2 * w, w:]
    h22, h00 = sums[2 * w :, 0:w], sums[2 * w :, w:]
    mul = functools.partial(nn, precision=HIGH)
    mul_t = functools.partial(nt, precision=HIGH)
    one = eye(w)
    y0 = one - STEP * h01.T
    part = mul(y0, h01)
    m1 = chol_inverse(mul_t(mul(y0, h00), y0) + STEP * (part + part.T) + STEP * STEP * h11)
    a0, a1 = mul(m1, y0), STEP * m1
    s01 = mul_t(h01, a0) + mul_t(h02, a1)
    s11 = mul_t(h11, a0) + mul_t(h12, a1)
    rayleigh = mul(a0, s01) + mul(a1, s11)
    turn = one - STEP * rayleigh.T
    b0 = mul(turn, a0) + MOMENTUM * (a0 - one)
    b1 = mul(turn, a1) + STEP * a0 + MOMENTUM * a1
    b2 = STEP * a1
    p01, p02, p12 = mul(b0, mul_t(h01, b1)), mul(b0, mul_t(h02, b2)), mul(b1, mul_t(h12, b2))
    mixed = p01 + p02 + p12
    square = mul(b0, mul_t(h00, b0)) + mul(b1, mul_t(h11, b1)) + mul(b2, mul_t(h22, b2))
    m2 = chol_inverse(square + (mixed + mixed.T))
    c0, c1, c2 = mul(m2, b0), mul(m2, b1), mul(m2, b2)
    coef[...] = jnp.zeros_like(coef)
    coef[0:w, 0:w] = c0
    coef[0:w, w : 2 * w] = c1
    coef[0:w, 2 * w : 3 * w] = c2
    coef[w:, 0:w] = c0 - a0
    coef[w:, w : 2 * w] = c1 - a1
    coef[w:, 2 * w : 3 * w] = c2


def small(points, gram):
    w = gram.shape[1] // 2
    here = pl.BlockSpec(memory_space=pltpu.VMEM)
    return pl.pallas_call(
        functools.partial(small_kernel, points),
        out_shape=jax.ShapeDtypeStruct((2 * w, 4 * w), f32),
        in_specs=[here],
        out_specs=here,
        scratch_shapes=Reduction.scratch(gram.shape[0]),
        compiler_params=pltpu.CompilerParams(collective_id=4, has_side_effects=True, vmem_limit_bytes=VM_LIMIT),
        name="small",
    )(gram)


def combine_kernel(coef, x0, t1, t2, basis, update):
    w = x0.shape[0]
    out = nn3(coef[:, 0 : 3 * w], jnp.concatenate([x0[...], t1[...], t2[...]], axis=0))
    basis[...] = out[:w]
    update[...] = out[w:]


def combine(coef, x0, t1, t2):
    w, owned = x0.shape
    chunk = 2048
    panel = pl.BlockSpec((w, chunk), lambda i: (0, i))
    return pl.pallas_call(
        combine_kernel,
        grid=(owned // chunk,),
        out_shape=(jax.ShapeDtypeStruct((w, owned), f32),) * 2,
        in_specs=[pl.BlockSpec(coef.shape, lambda i: (0, 0)), panel, panel, panel],
        out_specs=(panel, panel),
        compiler_params=pltpu.CompilerParams(vmem_limit_bytes=VM_LIMIT),
        name="combine",
    )(coef, x0, t1, t2)


def segments(key, rb):
    slots = key.shape[0]
    at = jnp.arange(slots, dtype=i32)
    mixed = key * slots + at
    rank = jnp.sum((mixed[None, :] < mixed[:, None]).astype(i32), axis=1)
    hit = (rank[None, :] == at[:, None]).astype(i32)
    order = jnp.sum(hit * at[None, :], axis=1)
    ranked = jnp.sum(hit * key[None, :], axis=1)
    before = jnp.concatenate([jnp.full((1,), -2, i32), ranked[:-1]])
    row = jnp.arange(rb, dtype=i32)
    last = jnp.sum((key[None, :] <= row[:, None]).astype(i32), axis=1) - 1
    any_here = jnp.max((key[None, :] == row[:, None]).astype(f32), axis=1)
    return order, (ranked == before).astype(f32), jnp.maximum(last, 0), any_here


def shards(diag_blocks, super_blocks, far_blocks, far_row, send_slot, panel):
    n = lax.axis_size("curve")
    rb, bs = diag_blocks.shape[:2]
    points = float(n * rb * bs)
    slots = far_row.shape[0]
    f_order, f_keep, f_last, f_any = segments(far_row, rb)
    s_order, s_keep, s_last, s_any = segments(send_slot, rb)

    def wide(x):
        return jnp.pad(x, (0, slots - x.shape[0]))

    index = jnp.stack(
        [jnp.maximum(send_slot, 0), jnp.maximum(far_row, 0), f_order, s_order, wide(f_last), wide(s_last)]
    )
    keep = jnp.stack([f_keep, s_keep, wide(f_any), wide(s_any)])
    x0, v0, root = start(n, diag_blocks, super_blocks, far_blocks, far_row, send_slot, panel)
    blocks = (diag_blocks, super_blocks, far_blocks)
    t1, u = exchange(n, (index, keep), v0, root, *blocks, ())
    t2, gram = exchange(n, (index, keep), u, root, *blocks, (x0, t1))
    return combine(small(points, gram), x0, t1, t2)


def solution(mesh):
    return jax.shard_map(
        shards,
        mesh=mesh,
        in_specs=(
            P("curve", None, None),
            P("curve", None, None, None),
            P("curve", None, None),
            P("curve"),
            P("curve"),
            P(None, "curve"),
        ),
        out_specs=(P(None, "curve"), P(None, "curve")),
        check_vma=False,
    )
```

```python
import functools

import jax
import jax.numpy as jnp
from jax import lax
from jax.experimental import pallas as pl
from jax.experimental.pallas import tpu as pltpu
from jax.sharding import PartitionSpec as P

f32, bf16, i32 = jnp.float32, jnp.bfloat16, jnp.int32
HIGH = lax.Precision.HIGHEST
STEP = 10.0
MOMENTUM = 0.5
MESH = pl.DeviceIdType.MESH
VMEM = pltpu.VMEM
DMA = pltpu.SemaphoreType.DMA
VM_LIMIT = 62 * 2**20


def nn(a, b, precision=None):
    return lax.dot_general(a, b, (((1,), (0,)), ((), ())), precision=precision, preferred_element_type=f32)


def nt(a, b, precision=None):
    return lax.dot_general(a, b, (((1,), (1,)), ((), ())), precision=precision, preferred_element_type=f32)


def halves(x):
    hi = x.astype(bf16)
    return hi, (x - hi.astype(f32)).astype(bf16)


def nn3(a, b):
    (ah, al), (bh, bl) = halves(a), halves(b)
    return nn(ah, bh) + (nn(ah, bl) + nn(al, bh))


def nt3(a, b):
    (ah, al), (bh, bl) = halves(a), halves(b)
    return nt(ah, bh) + (nt(ah, bl) + nt(al, bh))


def eye(n, m=None):
    m = m or n
    rows = lax.broadcasted_iota(i32, (n, m), 0)
    return (rows == lax.broadcasted_iota(i32, (n, m), 1)).astype(f32)


def chol_inverse(cross):
    n = cross.shape[0]
    both = jnp.concatenate([cross, eye(n)], axis=1)
    tiles = [both[8 * i : 8 * i + 8] for i in range(n // 8)]
    row_id = lax.broadcasted_iota(i32, (8, 1), 0)
    for k in range(n):
        at, sub = k // 8, k % 8
        row = tiles[at][sub : sub + 1]
        row = row / row[:, k : k + 1]
        for i in range(at, n // 8):
            column = tiles[i][:, k : k + 1]
            if i == at:
                column = jnp.where(row_id > sub, column, 0.0)
            tiles[i] = tiles[i] - column * row
    both = jnp.concatenate(tiles, axis=0)
    pivots = jnp.sum(both[:, :n] * eye(n), axis=1, keepdims=True)
    return both[:, n:] * lax.rsqrt(pivots)


def position():
    me = lax.axis_index("curve")
    return me, me // 32, (me // 8) % 4, (me // 2) % 4, me % 2


def partner(k):
    me, y, x, z, c = position()
    dz = (k // 2) % 4
    y, x, z, c = (y + k // 32 + dz) % 4, (x + k // 8 + dz) % 4, (z + dz) % 4, (c + k) % 2
    return ((y * 4 + x) * 4 + z) * 2 + c


def send(src, dst, ssem, rsem, to):
    copy = pltpu.make_async_remote_copy(
        src_ref=src, dst_ref=dst, send_sem=ssem, recv_sem=rsem, device_id=(to,), device_id_type=MESH
    )
    copy.start()
    return copy


def drain(ref, sem):
    pltpu.make_async_copy(ref, ref, sem).wait()


class Reduction:
    @staticmethod
    def scratch(rows):
        piece = rows // 8
        return [
            VMEM((8, piece, 128), f32),
            VMEM((8, piece, 128), f32),
            VMEM((16, piece, 128), f32),
            VMEM((8, piece, 128), f32),
            DMA((3,)),
            DMA((3,)),
        ]

    def __init__(self, refs):
        self.src, self.first, self.second, self.out, self.ss, self.rs = refs
        me = lax.axis_index("curve")
        self.sub = me % 8
        self.plane = me // 8

    def start(self, value):
        piece = value.shape[0] // 8
        for i in range(8):
            self.src[i] = value[i * piece : (i + 1) * piece]
        for k in range(1, 8):
            other = (self.sub + k) % 8
            send(self.src.at[other], self.first.at[self.sub], self.ss.at[0], self.rs.at[0], self.plane * 8 + other)
        self.first[self.sub] = self.src[self.sub]

    def across(self):
        drain(self.first.at[pl.ds(0, 7)], self.rs.at[0])
        total = self.first[0]
        for i in range(1, 8):
            total = total + self.first[i]
        self.second[self.plane] = total
        for k in range(1, 16):
            to = (self.plane + k) % 16 * 8 + self.sub
            send(self.second.at[self.plane], self.second.at[self.plane], self.ss.at[1], self.rs.at[1], to)

    def gather(self):
        drain(self.second.at[pl.ds(0, 15)], self.rs.at[1])
        parts = [self.second[i] for i in range(16)]
        while len(parts) > 1:
            parts = [a + b for a, b in zip(parts[::2], parts[1::2])]
        self.out[self.sub] = parts[0]
        for k in range(1, 8):
            to = self.plane * 8 + (self.sub + k) % 8
            send(self.out.at[self.sub], self.out.at[self.sub], self.ss.at[2], self.rs.at[2], to)

    def result(self):
        drain(self.out.at[pl.ds(0, 7)], self.rs.at[2])
        return jnp.concatenate([self.out[i] for i in range(8)], axis=0)

    def close(self):
        drain(self.src.at[pl.ds(0, 7)], self.ss.at[0])
        drain(self.second.at[pl.ds(0, 15)], self.ss.at[1])
        drain(self.out.at[pl.ds(0, 7)], self.ss.at[2])


def block(b):
    return pl.ds(pl.multiple_of(b * 128, 128), 128)


GROUPS = 4


def coefficients(gram, w):
    h01, h11 = gram[0:w, 0:w], gram[0:w, w:]
    h02, h12 = gram[w : 2 * w, 0:w], gram[w : 2 * w, w:]
    h22, h00 = gram[2 * w :, 0:w], gram[2 * w :, w:]
    mul = functools.partial(nn, precision=HIGH)
    mul_t = functools.partial(nt, precision=HIGH)
    one = eye(w)
    y0 = one - STEP * h01.T
    part = mul(y0, h01)
    m1 = chol_inverse(mul_t(mul(y0, h00), y0) + STEP * (part + part.T) + STEP * STEP * h11)
    a0, a1 = mul(m1, y0), STEP * m1
    s01 = mul_t(h01, a0) + mul_t(h02, a1)
    s11 = mul_t(h11, a0) + mul_t(h12, a1)
    rayleigh = mul(a0, s01) + mul(a1, s11)
    turn = one - STEP * rayleigh.T
    b0 = mul(turn, a0) + MOMENTUM * (a0 - one)
    b1 = mul(turn, a1) + STEP * a0 + MOMENTUM * a1
    b2 = STEP * a1
    p01, p02, p12 = mul(b0, mul_t(h01, b1)), mul(b0, mul_t(h02, b2)), mul(b1, mul_t(h12, b2))
    mixed = p01 + p02 + p12
    square = mul(b0, mul_t(h00, b0)) + mul(b1, mul_t(h11, b1)) + mul(b2, mul_t(h22, b2))
    m2 = chol_inverse(square + (mixed + mixed.T))
    c0, c1, c2 = mul(m2, b0), mul(m2, b1), mul(m2, b2)
    return (c0, c1, c2), (c0 - a0, c1 - a1, c2)


def whole_kernel(
    n, rb, bands, points,
    index, keep, index_v, spread, panel_hbm, diag_hbm, super_hbm, far_hbm,
    x_hbm, t1_hbm, t2_hbm, coef,
    diag, sup, far, x0, t1, t2, v, u, root, ahead, near, stage, mirror, seg, tails,
    deg, far_sums, cols, cols_in, deg_tail, load_sem, out_sem, small_sem, send_sem, recv_sem, *rest,
):
    width = x0.shape[0]
    slots = far.shape[0]
    part = slots // GROUPS
    owned = rb * 128
    per = n // GROUPS
    me = lax.axis_index("curve")
    panel = t2
    loads = [
        pltpu.make_async_copy(panel_hbm, panel, load_sem.at[0]),
        pltpu.make_async_copy(diag_hbm, diag, load_sem.at[1]),
        pltpu.make_async_copy(super_hbm, sup, load_sem.at[2]),
        pltpu.make_async_copy(far_hbm, far, load_sem.at[3]),
    ]
    for load in loads:
        load.start()
    barrier = pltpu.get_barrier_semaphore()

    @pl.loop(1, n)
    def _(k):
        pl.semaphore_signal(barrier, inc=1, device_id=(partner(k),), device_id_type=MESH)

    arrive, reductions = rest[: 4 * GROUPS], rest[4 * GROUPS :]
    came1, back1, came2, back2 = (arrive[i * GROUPS : (i + 1) * GROUPS] for i in range(4))
    first_sum, last_sum = Reduction(reductions[:6]), Reduction(reductions[6:])
    following, previous = (me + 1) % n, (me + n - 1) % n

    loads[0].wait()
    hi, lo = halves(panel[...])
    cross = nt(hi, lo)
    gram = nt(hi, hi) + (cross + cross.T)
    deg[...] = jnp.zeros_like(deg)
    ones = jnp.ones((16, 128), bf16)

    def row_sums(blk):
        return nt(ones, blk)[0:1]

    def column_sums(blk):
        return jnp.sum(blk.astype(f32), axis=0, keepdims=True)

    def near_degree(b, carry):
        rows = row_sums(diag[b]) + column_sums(diag[b])
        for h in range(bands):
            rows = rows + row_sums(sup[b, h])
            deg[pl.ds(b + h + 1, 1), :] += column_sums(sup[b, h])
        deg[pl.ds(b, 1), :] += rows
        return carry

    loads[1].wait()
    loads[2].wait()
    lax.fori_loop(0, rb // 2, near_degree, 0)
    pl.semaphore_wait(barrier, n - 1)
    first_sum.start(jnp.concatenate([gram, jnp.zeros_like(gram)], axis=1))
    lax.fori_loop(rb // 2, rb, near_degree, 0)
    first_sum.across()
    deg_sent = send(deg.at[pl.ds(rb, 8)], deg_tail, small_sem.at[0], small_sem.at[1], following)
    loads[3].wait()
    sub = lax.broadcasted_iota(i32, (8, 128), 0)

    def far_degree(k):
        t = partner(k)
        pair = []
        for c in range(2):
            f = 2 * t + c
            far_sums[pl.ds(f, 1), :] = row_sums(far[f])
            pair.append(column_sums(far[f]))
        cols[t] = jnp.where(sub == 0, pair[0], jnp.where(sub == 1, pair[1], 0.0))
        return t

    def far_step(k, carry):
        t = far_degree(k)
        send(cols.at[t], cols_in.at[me], small_sem.at[2], small_sem.at[3], t)
        return carry

    far_degree(0)
    cols_in[me] = cols[me]
    lax.fori_loop(1, n // 2, far_step, 0)
    first_sum.gather()
    lax.fori_loop(n // 2, n, far_step, 0)

    inverse = chol_inverse(first_sum.result()[:, :width] * (1.0 / points))
    x0[...] = nn3(inverse, panel[...])
    saves = [pltpu.make_async_copy(x0, x_hbm, out_sem.at[0])]
    saves[0].start()

    owner_rows = lax.broadcasted_iota(i32, (rb, slots), 0)
    degree = deg[0:rb, :] + nn((owner_rows == index_v[6:7, :]).astype(f32), far_sums[...], HIGH)
    deg_sent.wait_recv()
    degree = degree + jnp.concatenate([deg_tail[...], jnp.zeros((rb - 8, 128), f32)], axis=0)
    slot_rows = lax.broadcasted_iota(i32, (rb, 8 * n), 0)
    chosen = (slot_rows == spread[0:1, :]).astype(f32)
    drain(cols_in.at[pl.ds(0, n - 1)], small_sem.at[3])
    degree = degree + nn(chosen, cols_in[...].reshape(8 * n, 128), HIGH)
    root[...] = lax.rsqrt(degree)

    def scale(b, carry):
        v[b] = (x0[:, block(b)] * root[pl.ds(b, 1), :]).astype(bf16)
        return carry

    lax.fori_loop(0, rb, scale, 0, unroll=2)

    zero = jnp.zeros((width, 128), f32)

    def apply(turn, v, came, back, meanwhile, done):
        ss = [send_sem.at[4 * turn + i] for i in range(4)]
        rs = [recv_sem.at[10 * turn + i] for i in range(10)]
        halo = send(v.at[pl.ds(0, bands)], ahead.at[turn], ss[2], rs[8], previous)

        def stage_one(k):
            t = partner(k)
            for c in range(2):
                stage[2 * t + c] = v[index[0, 2 * t + c]]
            return t

        def mirror_one(k):
            t = partner(k)
            for c in range(2):
                f = 2 * t + c
                mirror[f] = nn(v[index[1, f]], far[f]).astype(bf16)
            return t

        def send_all(make, src, dst, ssem, rsems):
            make(0)
            dst[0][0:2] = src[pl.ds(2 * me, 2)]
            for g in range(GROUPS):

                def step(k, carry, g=g):
                    t = make(k)
                    send(src.at[pl.ds(2 * t, 2)], dst[g].at[pl.ds(2 * (k - g * per), 2)], ssem, rsems[g], t)
                    return carry

                lax.fori_loop(max(1, g * per), (g + 1) * per, step, 0)

        send_all(stage_one, stage, came, ss[0], rs[0:4])
        send_all(mirror_one, mirror, back, ss[1], rs[4:8])

        near[...] = jnp.zeros_like(near)

        def near_one(b, fetch):
            vb = v[b]
            out = nt(vb, diag[b]) + nn(vb, diag[b])
            for h in range(bands):
                out = out + nt(fetch(b + h + 1), sup[b, h])
                near[:, block(b + h + 1)] += nn(vb, sup[b, h])
            near[:, block(b)] += out

        def near_step(b, carry):
            near_one(b, lambda at: v[at])
            return carry

        lax.fori_loop(0, rb - bands, near_step, 0)
        halo.wait_recv()
        for b in range(rb - bands, rb):
            near_one(b, lambda at: v[at] if at < rb else ahead[turn, at - rb])
        tail = send(near.at[:, pl.ds(owned, bands * 128)], tails.at[turn], ss[3], rs[9], following)
        meanwhile()

        def arrived(ref, g, sem):
            drain(ref[g].at[pl.ds(0, part - 2 if g == 0 else part)], sem)

        for g in range(GROUPS):
            arrived(came, g, rs[g])

            def forward(i4, total, g=g):
                for i in range(4):
                    i1 = i4 * 4 + i
                    j = g * part + i1
                    total = total * keep[0, j] + nt(came[g][index[2, j]], far[index[7, j]])
                    seg[i1] = total
                return total

            lax.fori_loop(0, part // 4, forward, zero)

            def add_forward(b, carry, g=g):
                near[:, block(b)] += seg[index[4, g * rb + b]] * keep[2, g * rb + b]
                return carry

            lax.fori_loop(0, rb, add_forward, 0)
        tail.wait_recv()
        near[:, 0 : bands * 128] += tails[turn]
        for g in range(GROUPS):
            arrived(back, g, rs[4 + g])

            def backward(i4, total, g=g):
                for i in range(4):
                    i1 = i4 * 4 + i
                    j = g * part + i1
                    total = total * keep[1, j] + back[g][index[3, j]].astype(f32)
                    seg[i1] = total
                return total

            lax.fori_loop(0, part // 4, backward, zero)

            def add_backward(b, carry, g=g):
                total = near[:, block(b)] + seg[index[5, g * rb + b]] * keep[3, g * rb + b]
                if g < GROUPS - 1:
                    near[:, block(b)] = total
                else:
                    done(b, total)
                return carry

            lax.fori_loop(0, rb, add_backward, 0)
        halo.wait_send()
        tail.wait_send()
        drain(stage.at[pl.ds(0, slots - 2)], ss[0])
        drain(mirror.at[pl.ds(0, slots - 2)], ss[1])

    def first_done(b, total):
        d = root[pl.ds(b, 1), :]
        t = total * d
        t1[:, block(b)] = t
        u[b] = (t * d).astype(bf16)

    def last_done(b, total):
        t2[:, block(b)] = total * root[pl.ds(b, 1), :]

    apply(0, v, came1, back1, lambda: None, first_done)
    saves.append(pltpu.make_async_copy(t1, t1_hbm, out_sem.at[1]))
    saves[1].start()

    early = []

    def early_gram():
        (xh, xl), (ph, pl_) = halves(x0[...]), halves(t1[...])
        c00, c11 = nt(xh, xl), nt(ph, pl_)
        early.append(nt(xh, ph) + (nt(xh, pl_) + nt(xl, ph)))
        early.append(nt(ph, ph) + (c11 + c11.T))
        early.append(nt(xh, xh) + (c00 + c00.T))

    apply(1, u, came2, back2, early_gram, last_done)
    saves.append(pltpu.make_async_copy(t2, t2_hbm, out_sem.at[2]))
    saves[2].start()

    (th, tl), (xh, xl), (ph, pl_) = halves(t2[...]), halves(x0[...]), halves(t1[...])
    c22 = nt(th, tl)
    h01, h11, h00 = early
    h02 = nt(xh, th) + (nt(xh, tl) + nt(xl, th))
    h12 = nt(ph, th) + (nt(ph, tl) + nt(pl_, th))
    h22 = nt(th, th) + (c22 + c22.T)
    lanes = functools.partial(jnp.concatenate, axis=1)
    last_sum.start(jnp.concatenate([lanes([h01, h11]), lanes([h02, h12]), lanes([h22, h00])], axis=0))
    last_sum.across()
    last_sum.gather()
    new, change = coefficients(last_sum.result() * (1.0 / points), width)
    coef[...] = jnp.zeros_like(coef)
    for i in range(3):
        coef[0:width, i * width : (i + 1) * width] = new[i]
        coef[width:, i * width : (i + 1) * width] = change[i]
    for save in saves:
        save.wait()
    deg_sent.wait_send()
    drain(cols.at[pl.ds(0, n - 1)], small_sem.at[2])
    first_sum.close()
    last_sum.close()


def whole(n, tables, panel, diag_blocks, super_blocks, far_blocks):
    rb, bs = diag_blocks.shape[:2]
    bands, slots = super_blocks.shape[1], far_blocks.shape[0]
    width, owned = panel.shape
    index, keep, spread = tables
    here = pl.BlockSpec(memory_space=pltpu.VMEM)
    away = pl.BlockSpec(memory_space=pl.ANY)
    scalar = pl.BlockSpec(memory_space=pltpu.SMEM)
    wide = jax.ShapeDtypeStruct((width, owned), f32)
    blocks = VMEM((slots, width, bs), bf16)
    return pl.pallas_call(
        functools.partial(whole_kernel, n, rb, bands, float(n * owned)),
        out_shape=(wide, wide, wide, jax.ShapeDtypeStruct((2 * width, 4 * width), f32)),
        in_specs=[scalar, scalar, here, here, away, away, away, away],
        out_specs=(away, away, away, here),
        scratch_shapes=[
            VMEM(diag_blocks.shape, bf16),
            VMEM(super_blocks.shape, bf16),
            VMEM(far_blocks.shape, bf16),
            VMEM((width, owned), f32),
            VMEM((width, owned), f32),
            VMEM((width, owned), f32),
            VMEM((rb, width, bs), bf16),
            VMEM((rb, width, bs), bf16),
            VMEM((rb, bs), f32),
            VMEM((2, bands, width, bs), bf16),
            VMEM((width, owned + bands * bs), f32),
            *[blocks] * 2,
            VMEM((slots // GROUPS, width, bs), f32),
            VMEM((2, width, bands * bs), f32),
            VMEM((rb + 8, bs), f32),
            VMEM((slots, bs), f32),
            VMEM((n, 8, bs), f32),
            VMEM((n, 8, bs), f32),
            VMEM((8, bs), f32),
            DMA((4,)),
            DMA((3,)),
            DMA((4,)),
            DMA((8,)),
            DMA((20,)),
            *[VMEM((slots // GROUPS, width, bs), bf16)] * (4 * GROUPS),
            *Reduction.scratch(width),
            *Reduction.scratch(3 * width),
        ],
        compiler_params=pltpu.CompilerParams(collective_id=1, has_side_effects=True, vmem_limit_bytes=VM_LIMIT),
        name="whole",
    )(index, keep, index, spread, panel, diag_blocks, super_blocks, far_blocks)


def combine_kernel(coef, x0, t1, t2, basis, update):
    w = x0.shape[0]
    out = nn3(coef[:, 0 : 3 * w], jnp.concatenate([x0[...], t1[...], t2[...]], axis=0))
    basis[...] = out[:w]
    update[...] = out[w:]


def combine(coef, x0, t1, t2):
    w, owned = x0.shape
    chunk = 2048
    panel = pl.BlockSpec((w, chunk), lambda i: (0, i))
    return pl.pallas_call(
        combine_kernel,
        grid=(owned // chunk,),
        out_shape=(jax.ShapeDtypeStruct((w, owned), f32),) * 2,
        in_specs=[pl.BlockSpec(coef.shape, lambda i: (0, 0)), panel, panel, panel],
        out_specs=(panel, panel),
        compiler_params=pltpu.CompilerParams(vmem_limit_bytes=VM_LIMIT),
        name="combine",
    )(coef, x0, t1, t2)


def tables_kernel(n, rb, far_row, send_slot, index, keep, spread):
    slots = far_row.shape[1]
    part = slots // GROUPS
    _, y, x, z, c = position()
    lane = lax.broadcasted_iota(i32, (1, slots), 1)
    other = lane // 2
    dz = (z - (other // 2) % 4 + 4) % 4
    group = (y - other // 32 - dz + 8) % 4
    place = (((x - (other // 8) % 4 - dz + 8) % 4) * 8 + dz * 2 + (c + other) % 2) * 2 + lane % 2
    rows, lanes = (lax.broadcasted_iota(i32, (slots, slots), d) for d in (0, 1))
    same = rows == lanes
    send, far = send_slot[...], far_row[...]
    index[...] = jnp.zeros_like(index)
    keep[...] = jnp.zeros_like(keep)
    index[0:1] = jnp.maximum(send, 0)
    index[1:2] = jnp.maximum(far, 0)
    index[6:7] = far
    places = jnp.sum(jnp.where(same, jnp.broadcast_to(place, same.shape), 0), axis=1, keepdims=True)
    stride = rb + 2
    target = (lane // rb) * stride + lane % rb + 1
    for at, key in ((0, far), (1, send)):
        kind = group * stride + key + 1
        mixed = kind * slots + lane
        column = jnp.sum(jnp.where(same, jnp.broadcast_to(mixed, same.shape), 0), axis=1, keepdims=True)
        rank = jnp.sum((mixed < column).astype(i32), axis=1, keepdims=True)
        hit = rank == lanes
        ranked = jnp.sum(jnp.where(hit, jnp.broadcast_to(column, hit.shape), 0), axis=0, keepdims=True)
        order = jnp.sum(jnp.where(hit, jnp.broadcast_to(places, hit.shape), 0), axis=0, keepdims=True)
        if at == 0:
            index[7:8] = ranked % slots
        ranked = ranked // slots
        before = jnp.concatenate([jnp.full((1, 1), -1, i32), ranked[:, :-1]], axis=1)
        kinds = column // slots
        last = jnp.sum((kinds <= target).astype(i32), axis=0, keepdims=True) - 1
        found = jnp.sum((kinds == target).astype(i32), axis=0, keepdims=True)
        index[2 + at : 3 + at] = order
        index[4 + at : 5 + at] = jnp.clip(last - (lane // rb) * part, 0, part - 1)
        keep[at : at + 1] = jnp.where(lane % part == 0, 0.0, (ranked == before).astype(f32))
        keep[2 + at : 3 + at] = (found > 0).astype(f32)
    wide = lax.broadcasted_iota(i32, (slots, 8 * n), 1)
    slot = lax.broadcasted_iota(i32, (slots, 8 * n), 0)
    pairs = ((wide // 8 == slot // 2) & (wide % 8 == slot % 2)).astype(bf16)
    some = jnp.broadcast_to((send + 1).astype(f32), (16, slots)).astype(bf16)
    spread[...] = nn(some, pairs)[0:8].astype(i32) - 1


def tables_of(n, rb, far_row, send_slot):
    slots = far_row.shape[0]
    here = pl.BlockSpec(memory_space=pltpu.VMEM)
    return pl.pallas_call(
        functools.partial(tables_kernel, n, rb),
        out_shape=(
            jax.ShapeDtypeStruct((8, slots), i32),
            jax.ShapeDtypeStruct((8, slots), f32),
            jax.ShapeDtypeStruct((8, 8 * n), i32),
        ),
        in_specs=[here, here],
        out_specs=(here, here, here),
        name="tables",
    )(far_row.reshape(1, slots), send_slot.reshape(1, slots))


def shards(diag_blocks, super_blocks, far_blocks, far_row, send_slot, panel):
    n = lax.axis_size("curve")
    tables = tables_of(n, diag_blocks.shape[0], far_row, send_slot)
    x0, t1, t2, coef = whole(n, tables, panel, diag_blocks, super_blocks, far_blocks)
    return combine(coef, x0, t1, t2)


def solution(mesh):
    return jax.shard_map(
        shards,
        mesh=mesh,
        in_specs=(
            P("curve", None, None),
            P("curve", None, None, None),
            P("curve", None, None),
            P("curve"),
            P("curve"),
            P(None, "curve"),
        ),
        out_specs=(P(None, "curve"), P(None, "curve")),
        check_vma=False,
    )
```

```python
import functools

import jax
import jax.numpy as jnp
from jax import lax
from jax.experimental import pallas as pl
from jax.experimental.pallas import tpu as pltpu
from jax.sharding import PartitionSpec as P

f32, bf16, i32 = jnp.float32, jnp.bfloat16, jnp.int32
HIGH = lax.Precision.HIGHEST
STEP = 10.0
MOMENTUM = 0.5
MESH = pl.DeviceIdType.MESH
VMEM = pltpu.VMEM
DMA = pltpu.SemaphoreType.DMA
VM_LIMIT = 62 * 2**20


def nn(a, b, precision=None):
    return lax.dot_general(a, b, (((1,), (0,)), ((), ())), precision=precision, preferred_element_type=f32)


def nt(a, b, precision=None):
    return lax.dot_general(a, b, (((1,), (1,)), ((), ())), precision=precision, preferred_element_type=f32)


def halves(x):
    hi = x.astype(bf16)
    return hi, (x - hi.astype(f32)).astype(bf16)


def nn3(a, b):
    (ah, al), (bh, bl) = halves(a), halves(b)
    return nn(ah, bh) + (nn(ah, bl) + nn(al, bh))


def nt3(a, b):
    (ah, al), (bh, bl) = halves(a), halves(b)
    return nt(ah, bh) + (nt(ah, bl) + nt(al, bh))


def eye(n, m=None):
    m = m or n
    rows = lax.broadcasted_iota(i32, (n, m), 0)
    return (rows == lax.broadcasted_iota(i32, (n, m), 1)).astype(f32)


def chol_inverse(cross):
    n = cross.shape[0]
    both = jnp.concatenate([cross, eye(n)], axis=1)
    tiles = [both[8 * i : 8 * i + 8] for i in range(n // 8)]
    row_id = lax.broadcasted_iota(i32, (8, 1), 0)
    for k in range(n):
        at, sub = k // 8, k % 8
        row = tiles[at][sub : sub + 1]
        row = row / row[:, k : k + 1]
        for i in range(at, n // 8):
            column = tiles[i][:, k : k + 1]
            if i == at:
                column = jnp.where(row_id > sub, column, 0.0)
            tiles[i] = tiles[i] - column * row
    both = jnp.concatenate(tiles, axis=0)
    pivots = jnp.sum(both[:, :n] * eye(n), axis=1, keepdims=True)
    return both[:, n:] * lax.rsqrt(pivots)


def position():
    me = lax.axis_index("curve")
    return me, me // 32, (me // 8) % 4, (me // 2) % 4, me % 2


def partner(k):
    me, y, x, z, c = position()
    dz = (k // 2) % 4
    y, x, z, c = (y + k // 32 + dz) % 4, (x + k // 8 + dz) % 4, (z + dz) % 4, (c + k) % 2
    return ((y * 4 + x) * 4 + z) * 2 + c


def send(src, dst, ssem, rsem, to):
    copy = pltpu.make_async_remote_copy(
        src_ref=src, dst_ref=dst, send_sem=ssem, recv_sem=rsem, device_id=(to,), device_id_type=MESH
    )
    copy.start()
    return copy


def drain(ref, sem):
    pltpu.make_async_copy(ref, ref, sem).wait()


class Reduction:
    @staticmethod
    def scratch(rows):
        piece = rows // 8
        return [
            VMEM((8, piece, 128), f32),
            VMEM((8, piece, 128), f32),
            VMEM((16, piece, 128), f32),
            VMEM((8, piece, 128), f32),
            DMA((3,)),
            DMA((3,)),
        ]

    def __init__(self, refs):
        self.src, self.first, self.second, self.out, self.ss, self.rs = refs
        me = lax.axis_index("curve")
        self.sub = me % 8
        self.plane = me // 8

    def start(self, value):
        piece = value.shape[0] // 8
        for i in range(8):
            self.src[i] = value[i * piece : (i + 1) * piece]
        for k in range(1, 8):
            other = (self.sub + k) % 8
            send(self.src.at[other], self.first.at[self.sub], self.ss.at[0], self.rs.at[0], self.plane * 8 + other)
        self.first[self.sub] = self.src[self.sub]

    def across(self):
        drain(self.first.at[pl.ds(0, 7)], self.rs.at[0])
        total = self.first[0]
        for i in range(1, 8):
            total = total + self.first[i]
        self.second[self.plane] = total
        for k in range(1, 16):
            to = (self.plane + k) % 16 * 8 + self.sub
            send(self.second.at[self.plane], self.second.at[self.plane], self.ss.at[1], self.rs.at[1], to)

    def gather(self):
        drain(self.second.at[pl.ds(0, 15)], self.rs.at[1])
        parts = [self.second[i] for i in range(16)]
        while len(parts) > 1:
            parts = [a + b for a, b in zip(parts[::2], parts[1::2])]
        self.out[self.sub] = parts[0]
        for k in range(1, 8):
            to = self.plane * 8 + (self.sub + k) % 8
            send(self.out.at[self.sub], self.out.at[self.sub], self.ss.at[2], self.rs.at[2], to)

    def result(self):
        drain(self.out.at[pl.ds(0, 7)], self.rs.at[2])
        return jnp.concatenate([self.out[i] for i in range(8)], axis=0)

    def close(self):
        drain(self.src.at[pl.ds(0, 7)], self.ss.at[0])
        drain(self.second.at[pl.ds(0, 15)], self.ss.at[1])
        drain(self.out.at[pl.ds(0, 7)], self.ss.at[2])


def block(b):
    return pl.ds(pl.multiple_of(b * 128, 128), 128)


GROUPS = 4


mul = functools.partial(nn, precision=HIGH)
mul_t = functools.partial(nt, precision=HIGH)


def first_step(h00, h01, h11):
    y0 = eye(h00.shape[0]) - STEP * h01.T
    part = mul(y0, h01)
    m1 = chol_inverse(mul_t(mul(y0, h00), y0) + STEP * (part + part.T) + STEP * STEP * h11)
    return mul(m1, y0), STEP * m1


def second_step(h00, h01, h11, a0, a1, h02, h12, h22):
    one = eye(h00.shape[0])
    s01 = mul_t(h01, a0) + mul_t(h02, a1)
    s11 = mul_t(h11, a0) + mul_t(h12, a1)
    rayleigh = mul(a0, s01) + mul(a1, s11)
    turn = one - STEP * rayleigh.T
    b0 = mul(turn, a0) + MOMENTUM * (a0 - one)
    b1 = mul(turn, a1) + STEP * a0 + MOMENTUM * a1
    b2 = STEP * a1
    p01, p02, p12 = mul(b0, mul_t(h01, b1)), mul(b0, mul_t(h02, b2)), mul(b1, mul_t(h12, b2))
    mixed = p01 + p02 + p12
    square = mul(b0, mul_t(h00, b0)) + mul(b1, mul_t(h11, b1)) + mul(b2, mul_t(h22, b2))
    m2 = chol_inverse(square + (mixed + mixed.T))
    c0, c1, c2 = mul(m2, b0), mul(m2, b1), mul(m2, b2)
    return (c0, c1, c2), (c0 - a0, c1 - a1, c2)


def whole_kernel(
    n, rb, bands, points,
    index, keep, index_v, panel_hbm, diag_hbm, super_hbm, far_hbm,
    x_hbm, t1_hbm, t2_hbm, coef,
    diag, sup, far, x0, t1, t2, v, u, root, ahead, near, stage, mirror, seg, tails,
    deg, far_sums, cols, cols_in, deg_tail, load_sem, out_sem, small_sem, send_sem, recv_sem, *rest,
):
    width = x0.shape[0]
    slots = far.shape[0]
    part = slots // GROUPS
    owned = rb * 128
    per = n // GROUPS
    me = lax.axis_index("curve")
    panel = t2
    loads = [
        pltpu.make_async_copy(panel_hbm, panel, load_sem.at[0]),
        pltpu.make_async_copy(diag_hbm, diag, load_sem.at[1]),
        pltpu.make_async_copy(super_hbm, sup, load_sem.at[2]),
        pltpu.make_async_copy(far_hbm, far, load_sem.at[3]),
    ]
    for load in loads:
        load.start()
    barrier = pltpu.get_barrier_semaphore()

    @pl.loop(1, n)
    def _(k):
        pl.semaphore_signal(barrier, inc=1, device_id=((me + k) % n,), device_id_type=MESH)

    arrive, reductions = rest[: 4 * GROUPS], rest[4 * GROUPS :]
    came1, back1, came2, back2 = (arrive[i * GROUPS : (i + 1) * GROUPS] for i in range(4))
    first_sum, mid_sum, last_sum = (Reduction(reductions[i : i + 6]) for i in (0, 6, 12))
    following, previous = (me + 1) % n, (me + n - 1) % n

    loads[0].wait()
    hi, lo = halves(panel[...])
    cross = nt(hi, lo)
    gram = nt(hi, hi) + (cross + cross.T)
    deg[...] = jnp.zeros_like(deg)
    ones = jnp.ones((16, 128), bf16)

    def row_sums(blk):
        return nt(ones, blk)[0:1]

    def column_sums(blk):
        return jnp.sum(blk.astype(f32), axis=0, keepdims=True)

    def near_degree(b, carry):
        rows = row_sums(diag[b]) + column_sums(diag[b])
        for h in range(bands):
            rows = rows + row_sums(sup[b, h])
            deg[pl.ds(b + h + 1, 1), :] += column_sums(sup[b, h])
        deg[pl.ds(b, 1), :] += rows
        return carry

    loads[1].wait()
    loads[2].wait()
    lax.fori_loop(0, rb // 2, near_degree, 0, unroll=4)
    pl.semaphore_wait(barrier, n - 1)
    first_sum.start(jnp.concatenate([gram, jnp.zeros_like(gram)], axis=1))
    lax.fori_loop(rb // 2, rb, near_degree, 0, unroll=4)
    first_sum.across()
    deg_sent = send(deg.at[pl.ds(rb, 8)], deg_tail, small_sem.at[0], small_sem.at[1], following)
    loads[3].wait()

    def far_degree(k):
        t = partner(k)
        for c in range(2):
            f = 2 * t + c
            far_sums[pl.ds(f, 1), :] = row_sums(far[f])
            cols[f] = column_sums(far[f])
        return t

    def far_step(k, carry):
        t = far_degree(k)
        send(cols.at[pl.ds(2 * t, 2)], cols_in.at[pl.ds(2 * me, 2)], small_sem.at[2], small_sem.at[3], t)
        return carry

    far_degree(0)
    cols_in[pl.ds(2 * me, 2)] = cols[pl.ds(2 * me, 2)]
    lax.fori_loop(1, n // 2 + 1, far_step, 0, unroll=4)
    first_sum.gather()
    lax.fori_loop(n // 2 + 1, n, far_step, 0, unroll=3)

    gram = first_sum.result()[:, :width] * (1.0 / points)
    inverse = chol_inverse(gram)
    h00 = mul_t(mul(inverse, gram), inverse)
    x0[...] = nn3(inverse, panel[...])
    saves = [pltpu.make_async_copy(x0, x_hbm, out_sem.at[0])]
    saves[0].start()

    owner_rows = lax.broadcasted_iota(i32, (rb, slots), 0)
    degree = deg[0:rb, :] + nn((owner_rows == index_v[6:7, :]).astype(f32), far_sums[...], HIGH)
    deg_sent.wait_recv()
    degree = degree + jnp.concatenate([deg_tail[...], jnp.zeros((rb - 8, 128), f32)], axis=0)
    slot_rows = lax.broadcasted_iota(i32, (rb, slots), 0)
    chosen = (slot_rows == index_v[8:9, :]).astype(f32)
    drain(cols_in.at[pl.ds(0, slots - 2)], small_sem.at[3])

    def unpack(f, carry):
        far_sums[pl.ds(f, 1), :] = cols_in[f]
        return carry

    lax.fori_loop(0, slots, unpack, 0, unroll=8)
    degree = degree + nn(chosen, far_sums[...], HIGH)
    root[...] = lax.rsqrt(degree)

    def scale(b, carry):
        v[b] = (x0[:, block(b)] * root[pl.ds(b, 1), :]).astype(bf16)
        return carry

    lax.fori_loop(0, rb, scale, 0, unroll=2)

    zero = jnp.zeros((width, 128), f32)

    def apply(turn, v, came, back, hooks, done):
        ss = [send_sem.at[4 * turn + i] for i in range(4)]
        rs = [recv_sem.at[10 * turn + i] for i in range(10)]
        halo = send(v.at[pl.ds(0, bands)], ahead.at[turn], ss[2], rs[8], previous)

        def stage_one(k):
            t = partner(k)
            for c in range(2):
                stage[2 * t + c] = v[index[0, 2 * t + c]]
            return t

        def mirror_one(k):
            t = partner(k)
            for c in range(2):
                f = 2 * t + c
                mirror[f] = nn(v[index[1, f]], far[f]).astype(bf16)
            return t

        def send_groups(make, src, dst, ssem, rsems, groups):
            if 0 in groups:
                make(0)
                dst[0][0:2] = src[pl.ds(2 * me, 2)]
            for g in groups:

                def step(k, carry, g=g):
                    t = make(k)
                    send(src.at[pl.ds(2 * t, 2)], dst[g].at[pl.ds(2 * (k - g * per), 2)], ssem, rsems[g], t)
                    return carry

                lax.fori_loop(max(1, g * per), (g + 1) * per, step, 0)

        hooks[0]()
        send_groups(stage_one, stage, came, ss[0], rs[0:4], range(GROUPS))
        hooks[1]()
        send_groups(mirror_one, mirror, back, ss[1], rs[4:8], range(GROUPS // 2))

        near[...] = jnp.zeros_like(near)

        def near_one(b, fetch):
            vb = v[b]
            out = nt(vb, diag[b]) + nn(vb, diag[b])
            for h in range(bands):
                out = out + nt(fetch(b + h + 1), sup[b, h])
                near[:, block(b + h + 1)] += nn(vb, sup[b, h])
            near[:, block(b)] += out

        def near_step(b, carry):
            near_one(b, lambda at: v[at])
            return carry

        lax.fori_loop(0, rb - bands, near_step, 0)
        halo.wait_recv()
        for b in range(rb - bands, rb):
            near_one(b, lambda at: v[at] if at < rb else ahead[turn, at - rb])
        tail = send(near.at[:, pl.ds(owned, bands * 128)], tails.at[turn], ss[3], rs[9], following)
        hooks[2]()
        send_groups(mirror_one, mirror, back, ss[1], rs[4:8], range(GROUPS // 2, GROUPS))

        def arrived(ref, g, sem):
            drain(ref[g].at[pl.ds(0, part - 2 if g == 0 else part)], sem)

        for g in range(GROUPS):
            arrived(came, g, rs[g])

            def forward(i4, total, g=g):
                for i in range(4):
                    i1 = i4 * 4 + i
                    j = g * part + i1
                    total = total * keep[0, j] + nt(came[g][index[2, j]], far[index[7, j]])
                    seg[i1] = total
                return total

            lax.fori_loop(0, part // 4, forward, zero)

            def add_forward(b, carry, g=g):
                near[:, block(b)] += seg[index[4, g * rb + b]] * keep[2, g * rb + b]
                return carry

            lax.fori_loop(0, rb, add_forward, 0)
        tail.wait_recv()
        near[:, 0 : bands * 128] += tails[turn]
        hooks[3]()
        for g in range(GROUPS):
            arrived(back, g, rs[4 + g])

            def backward(i4, total, g=g):
                for i in range(4):
                    i1 = i4 * 4 + i
                    j = g * part + i1
                    total = total * keep[1, j] + back[g][index[3, j]].astype(f32)
                    seg[i1] = total
                return total

            lax.fori_loop(0, part // 4, backward, zero)

            def add_backward(b, carry, g=g):
                total = near[:, block(b)] + seg[index[5, g * rb + b]] * keep[3, g * rb + b]
                if g < GROUPS - 1:
                    near[:, block(b)] = total
                else:
                    done(b, total)
                return carry

            lax.fori_loop(0, rb, add_backward, 0, unroll=4)
        halo.wait_send()
        tail.wait_send()
        drain(stage.at[pl.ds(0, slots - 2)], ss[0])
        drain(mirror.at[pl.ds(0, slots - 2)], ss[1])

    def first_done(b, total):
        d = root[pl.ds(b, 1), :]
        t = total * d
        t1[:, block(b)] = t
        u[b] = (t * d).astype(bf16)

    def last_done(b, total):
        t2[:, block(b)] = total * root[pl.ds(b, 1), :]

    apply(0, v, came1, back1, [lambda: None] * 4, first_done)
    saves.append(pltpu.make_async_copy(t1, t1_hbm, out_sem.at[1]))
    saves[1].start()

    kept = []
    lanes = functools.partial(jnp.concatenate, axis=1)

    def early_gram():
        (xh, xl), (ph, pl_) = halves(x0[...]), halves(t1[...])
        c11 = nt(ph, pl_)
        h01 = nt(xh, ph) + (nt(xh, pl_) + nt(xl, ph))
        mid_sum.start(lanes([h01, nt(ph, ph) + (c11 + c11.T)]))

    def early_step():
        sums = mid_sum.result() * (1.0 / points)
        h01, h11 = sums[:, :width], sums[:, width:]
        kept.extend((h00, h01, h11, *first_step(h00, h01, h11)))

    apply(1, u, came2, back2, [early_gram, mid_sum.across, mid_sum.gather, early_step], last_done)
    saves.append(pltpu.make_async_copy(t2, t2_hbm, out_sem.at[2]))
    saves[2].start()

    (th, tl), (xh, xl), (ph, pl_) = halves(t2[...]), halves(x0[...]), halves(t1[...])
    c22 = nt(th, tl)
    h02 = nt(xh, th) + (nt(xh, tl) + nt(xl, th))
    h12 = nt(ph, th) + (nt(ph, tl) + nt(pl_, th))
    h22 = nt(th, th) + (c22 + c22.T)
    last_sum.start(jnp.concatenate([lanes([h02, h12]), lanes([h22, jnp.zeros_like(h22)])], axis=0))
    last_sum.across()
    last_sum.gather()
    sums = last_sum.result() * (1.0 / points)
    new, change = second_step(*kept, sums[:width, :width], sums[:width, width:], sums[width:, :width])
    coef[...] = jnp.zeros_like(coef)
    for i in range(3):
        coef[0:width, i * width : (i + 1) * width] = new[i]
        coef[width:, i * width : (i + 1) * width] = change[i]
    for save in saves:
        save.wait()
    deg_sent.wait_send()
    drain(cols.at[pl.ds(0, slots - 2)], small_sem.at[2])
    first_sum.close()
    mid_sum.close()
    last_sum.close()


def whole(n, tables, panel, diag_blocks, super_blocks, far_blocks):
    rb, bs = diag_blocks.shape[:2]
    bands, slots = super_blocks.shape[1], far_blocks.shape[0]
    width, owned = panel.shape
    index, keep = tables
    here = pl.BlockSpec(memory_space=pltpu.VMEM)
    away = pl.BlockSpec(memory_space=pl.ANY)
    scalar = pl.BlockSpec(memory_space=pltpu.SMEM)
    wide = jax.ShapeDtypeStruct((width, owned), f32)
    blocks = VMEM((slots, width, bs), bf16)
    return pl.pallas_call(
        functools.partial(whole_kernel, n, rb, bands, float(n * owned)),
        out_shape=(wide, wide, wide, jax.ShapeDtypeStruct((2 * width, 4 * width), f32)),
        in_specs=[scalar, scalar, here, away, away, away, away],
        out_specs=(away, away, away, here),
        scratch_shapes=[
            VMEM(diag_blocks.shape, bf16),
            VMEM(super_blocks.shape, bf16),
            VMEM(far_blocks.shape, bf16),
            VMEM((width, owned), f32),
            VMEM((width, owned), f32),
            VMEM((width, owned), f32),
            VMEM((rb, width, bs), bf16),
            VMEM((rb, width, bs), bf16),
            VMEM((rb, bs), f32),
            VMEM((2, bands, width, bs), bf16),
            VMEM((width, owned + bands * bs), f32),
            *[blocks] * 2,
            VMEM((slots // GROUPS, width, bs), f32),
            VMEM((2, width, bands * bs), f32),
            VMEM((rb + 8, bs), f32),
            VMEM((slots, bs), f32),
            VMEM((slots, 1, bs), f32),
            VMEM((slots, 1, bs), f32),
            VMEM((8, bs), f32),
            DMA((4,)),
            DMA((3,)),
            DMA((4,)),
            DMA((8,)),
            DMA((20,)),
            *[VMEM((slots // GROUPS, width, bs), bf16)] * (4 * GROUPS),
            *Reduction.scratch(width),
            *Reduction.scratch(width),
            *Reduction.scratch(2 * width),
        ],
        compiler_params=pltpu.CompilerParams(collective_id=1, has_side_effects=True, vmem_limit_bytes=VM_LIMIT),
        name="whole",
    )(index, keep, index, panel, diag_blocks, super_blocks, far_blocks)


def combine_kernel(coef, x0, t1, t2, basis, update):
    w = x0.shape[0]
    out = nn3(coef[:, 0 : 3 * w], jnp.concatenate([x0[...], t1[...], t2[...]], axis=0))
    basis[...] = out[:w]
    update[...] = out[w:]


def combine(coef, x0, t1, t2):
    w, owned = x0.shape
    chunk = 1024
    panel = pl.BlockSpec((w, chunk), lambda i: (0, i))
    return pl.pallas_call(
        combine_kernel,
        grid=(owned // chunk,),
        out_shape=(jax.ShapeDtypeStruct((w, owned), f32),) * 2,
        in_specs=[pl.BlockSpec(coef.shape, lambda i: (0, 0)), panel, panel, panel],
        out_specs=(panel, panel),
        compiler_params=pltpu.CompilerParams(vmem_limit_bytes=VM_LIMIT),
        name="combine",
    )(coef, x0, t1, t2)


def tables_kernel(n, rb, far_row, send_slot, index, keep):
    slots = far_row.shape[1]
    part = slots // GROUPS
    _, y, x, z, c = position()
    lane = lax.broadcasted_iota(i32, (1, slots), 1)
    other = lane // 2
    dz = (z - (other // 2) % 4 + 4) % 4
    group = (y - other // 32 - dz + 8) % 4
    place = (((x - (other // 8) % 4 - dz + 8) % 4) * 8 + dz * 2 + (c + other) % 2) * 2 + lane % 2
    rows, lanes = (lax.broadcasted_iota(i32, (slots, slots), d) for d in (0, 1))
    same = rows == lanes
    send, far = send_slot[...], far_row[...]
    index[...] = jnp.zeros_like(index)
    keep[...] = jnp.zeros_like(keep)
    index[0:1] = jnp.maximum(send, 0)
    index[1:2] = jnp.maximum(far, 0)
    index[6:7] = far
    index[8:9] = send
    places = jnp.sum(jnp.where(same, jnp.broadcast_to(place, same.shape), 0), axis=1, keepdims=True)
    stride = rb + 2
    target = (lane // rb) * stride + lane % rb + 1
    for at, key in ((0, far), (1, send)):
        kind = group * stride + key + 1
        mixed = kind * slots + lane
        column = jnp.sum(jnp.where(same, jnp.broadcast_to(mixed, same.shape), 0), axis=1, keepdims=True)
        rank = jnp.sum((mixed < column).astype(i32), axis=1, keepdims=True)
        hit = rank == lanes
        ranked = jnp.sum(jnp.where(hit, jnp.broadcast_to(column, hit.shape), 0), axis=0, keepdims=True)
        order = jnp.sum(jnp.where(hit, jnp.broadcast_to(places, hit.shape), 0), axis=0, keepdims=True)
        if at == 0:
            index[7:8] = ranked % slots
        ranked = ranked // slots
        before = jnp.concatenate([jnp.full((1, 1), -1, i32), ranked[:, :-1]], axis=1)
        kinds = column // slots
        last = jnp.sum((kinds <= target).astype(i32), axis=0, keepdims=True) - 1
        found = jnp.sum((kinds == target).astype(i32), axis=0, keepdims=True)
        index[2 + at : 3 + at] = order
        index[4 + at : 5 + at] = jnp.clip(last - (lane // rb) * part, 0, part - 1)
        keep[at : at + 1] = jnp.where(lane % part == 0, 0.0, (ranked == before).astype(f32))
        keep[2 + at : 3 + at] = (found > 0).astype(f32)


def tables_of(n, rb, far_row, send_slot):
    slots = far_row.shape[0]
    here = pl.BlockSpec(memory_space=pltpu.VMEM)
    return pl.pallas_call(
        functools.partial(tables_kernel, n, rb),
        out_shape=(
            jax.ShapeDtypeStruct((16, slots), i32),
            jax.ShapeDtypeStruct((8, slots), f32),
        ),
        in_specs=[here, here],
        out_specs=(here, here),
        name="tables",
    )(far_row.reshape(1, slots), send_slot.reshape(1, slots))


def shards(diag_blocks, super_blocks, far_blocks, far_row, send_slot, panel):
    n = lax.axis_size("curve")
    tables = tables_of(n, diag_blocks.shape[0], far_row, send_slot)
    x0, t1, t2, coef = whole(n, tables, panel, diag_blocks, super_blocks, far_blocks)
    return combine(coef, x0, t1, t2)


def solution(mesh):
    return jax.shard_map(
        shards,
        mesh=mesh,
        in_specs=(
            P("curve", None, None),
            P("curve", None, None, None),
            P("curve", None, None),
            P("curve"),
            P("curve"),
            P(None, "curve"),
        ),
        out_specs=(P(None, "curve"), P(None, "curve")),
        check_vma=False,
    )
```

```python
import functools

import jax
import jax.numpy as jnp
from jax import lax
from jax.experimental import pallas as pl
from jax.experimental.pallas import tpu as pltpu
from jax.sharding import PartitionSpec as P

f32, bf16, i32 = jnp.float32, jnp.bfloat16, jnp.int32
HIGH = lax.Precision.HIGHEST
STEP = 10.0
MOMENTUM = 0.5
MESH = pl.DeviceIdType.MESH
VMEM = pltpu.VMEM
DMA = pltpu.SemaphoreType.DMA
VM_LIMIT = 62 * 2**20


def nn(a, b, precision=None):
    return lax.dot_general(a, b, (((1,), (0,)), ((), ())), precision=precision, preferred_element_type=f32)


def nt(a, b, precision=None):
    return lax.dot_general(a, b, (((1,), (1,)), ((), ())), precision=precision, preferred_element_type=f32)


def halves(x):
    hi = x.astype(bf16)
    return hi, (x - hi.astype(f32)).astype(bf16)


def nn3(a, b):
    (ah, al), (bh, bl) = halves(a), halves(b)
    return nn(ah, bh) + (nn(ah, bl) + nn(al, bh))


def nt3(a, b):
    (ah, al), (bh, bl) = halves(a), halves(b)
    return nt(ah, bh) + (nt(ah, bl) + nt(al, bh))


def eye(n, m=None):
    m = m or n
    rows = lax.broadcasted_iota(i32, (n, m), 0)
    return (rows == lax.broadcasted_iota(i32, (n, m), 1)).astype(f32)


def chol_inverse(cross):
    n = cross.shape[0]
    rows, lanes = (lax.broadcasted_iota(i32, (n, n), d) for d in (0, 1))
    diagonal = jnp.where(rows == lanes, cross, 0.0)
    down = lax.rsqrt(jnp.sum(diagonal, axis=1, keepdims=True))
    along = lax.rsqrt(jnp.sum(diagonal, axis=0, keepdims=True))
    both = jnp.concatenate([cross * down * along, eye(n)], axis=1)
    tiles = [both[8 * i : 8 * i + 8] for i in range(n // 8)]
    row_id = lax.broadcasted_iota(i32, (8, 1), 0)
    for k in range(0, n, 2):
        at, sub = k // 8, k % 8
        r0, r1 = tiles[at][sub : sub + 1], tiles[at][sub + 1 : sub + 2]
        a, b, d = r0[:, k : k + 1], r0[:, k + 1 : k + 2], r1[:, k + 1 : k + 2]
        scale = 1.0 / (a * d - b * b)
        p0, p1 = (d * r0 - b * r1) * scale, (a * r1 - b * r0) * scale
        for i in range(at, n // 8):
            if i == at and sub == 6:
                continue
            c0, c1 = tiles[i][:, k : k + 1], tiles[i][:, k + 1 : k + 2]
            if i == at:
                c0, c1 = (jnp.where(row_id > sub + 1, c, 0.0) for c in (c0, c1))
            tiles[i] = tiles[i] - (c0 * p0 + c1 * p1)
    both = jnp.concatenate(tiles, axis=0)
    left, right = both[:, :n], both[:, n:]
    odd = lax.broadcasted_iota(i32, (n, 1), 0) % 2 == 1
    own = jnp.sum(jnp.where(rows == lanes, left, 0.0), axis=1, keepdims=True)
    side = jnp.sum(jnp.where(rows == lanes + 1, left, 0.0), axis=1, keepdims=True)
    above = jnp.concatenate([own[:1], own[:-1]], axis=0)
    ratio = jnp.where(odd, side / above, 0.0)
    upper = jnp.concatenate([right[:1], right[:-1]], axis=0)
    return (right - ratio * upper) * lax.rsqrt(own - ratio * side) * along


def position():
    me = lax.axis_index("curve")
    return me, me // 32, (me // 8) % 4, (me // 2) % 4, me % 2


def partner(k):
    me, y, x, z, c = position()
    dz = (k // 2) % 4
    y, x, z, c = (y + k // 32 + dz) % 4, (x + k // 8 + dz) % 4, (z + dz) % 4, (c + k) % 2
    return ((y * 4 + x) * 4 + z) * 2 + c


def send(src, dst, ssem, rsem, to):
    copy = pltpu.make_async_remote_copy(
        src_ref=src, dst_ref=dst, send_sem=ssem, recv_sem=rsem, device_id=(to,), device_id_type=MESH
    )
    copy.start()
    return copy


def drain(ref, sem):
    pltpu.make_async_copy(ref, ref, sem).wait()


class Reduction:
    @staticmethod
    def scratch(rows):
        piece = rows // 8
        return [
            VMEM((8, piece, 128), f32),
            VMEM((8, piece, 128), f32),
            VMEM((16, piece, 128), f32),
            VMEM((8, piece, 128), f32),
            DMA((3,)),
            DMA((3,)),
        ]

    def __init__(self, refs):
        self.src, self.first, self.second, self.out, self.ss, self.rs = refs
        me = lax.axis_index("curve")
        self.sub = me % 8
        self.plane = me // 8

    def start(self, value):
        piece = value.shape[0] // 8
        for i in range(8):
            self.src[i] = value[i * piece : (i + 1) * piece]
        for k in range(1, 8):
            other = (self.sub + k) % 8
            send(self.src.at[other], self.first.at[self.sub], self.ss.at[0], self.rs.at[0], self.plane * 8 + other)
        self.first[self.sub] = self.src[self.sub]

    def across(self):
        drain(self.first.at[pl.ds(0, 7)], self.rs.at[0])
        total = self.first[0]
        for i in range(1, 8):
            total = total + self.first[i]
        self.second[self.plane] = total
        for k in range(1, 16):
            to = (self.plane + k) % 16 * 8 + self.sub
            send(self.second.at[self.plane], self.second.at[self.plane], self.ss.at[1], self.rs.at[1], to)

    def gather(self):
        drain(self.second.at[pl.ds(0, 15)], self.rs.at[1])
        parts = [self.second[i] for i in range(16)]
        while len(parts) > 1:
            parts = [a + b for a, b in zip(parts[::2], parts[1::2])]
        self.out[self.sub] = parts[0]
        for k in range(1, 8):
            to = self.plane * 8 + (self.sub + k) % 8
            send(self.out.at[self.sub], self.out.at[self.sub], self.ss.at[2], self.rs.at[2], to)

    def result(self):
        drain(self.out.at[pl.ds(0, 7)], self.rs.at[2])
        return jnp.concatenate([self.out[i] for i in range(8)], axis=0)

    def close(self):
        drain(self.src.at[pl.ds(0, 7)], self.ss.at[0])
        drain(self.second.at[pl.ds(0, 15)], self.ss.at[1])
        drain(self.out.at[pl.ds(0, 7)], self.ss.at[2])


def block(b):
    return pl.ds(pl.multiple_of(b * 128, 128), 128)


GROUPS = 4


mul = functools.partial(nn, precision=HIGH)
mul_t = functools.partial(nt, precision=HIGH)


def first_step(h00, h01, h11):
    y0 = eye(h00.shape[0]) - STEP * h01.T
    part = mul(y0, h01)
    m1 = chol_inverse(mul_t(mul(y0, h00), y0) + STEP * (part + part.T) + STEP * STEP * h11)
    return mul(m1, y0), STEP * m1


def second_step(h00, h01, h11, a0, a1, h02, h12, h22):
    one = eye(h00.shape[0])
    s01 = mul_t(h01, a0) + mul_t(h02, a1)
    s11 = mul_t(h11, a0) + mul_t(h12, a1)
    rayleigh = mul(a0, s01) + mul(a1, s11)
    turn = one - STEP * rayleigh.T
    b0 = mul(turn, a0) + MOMENTUM * (a0 - one)
    b1 = mul(turn, a1) + STEP * a0 + MOMENTUM * a1
    b2 = STEP * a1
    p01, p02, p12 = mul(b0, mul_t(h01, b1)), mul(b0, mul_t(h02, b2)), mul(b1, mul_t(h12, b2))
    mixed = p01 + p02 + p12
    square = mul(b0, mul_t(h00, b0)) + mul(b1, mul_t(h11, b1)) + mul(b2, mul_t(h22, b2))
    m2 = chol_inverse(square + (mixed + mixed.T))
    c0, c1, c2 = mul(m2, b0), mul(m2, b1), mul(m2, b2)
    return (c0, c1, c2), (c0 - a0, c1 - a1, c2)


def whole_kernel(
    n, rb, bands, points,
    index, keep, index_v, panel_hbm, diag_hbm, super_hbm, far_hbm,
    x_hbm, t1_hbm, t2_hbm, coef,
    diag, sup, far, x0, t1, t2, v, u, root, ahead, near, stage, mirror, seg, tails,
    deg, far_sums, cols, cols_in, deg_tail, load_sem, out_sem, small_sem, send_sem, recv_sem, *rest,
):
    width = x0.shape[0]
    slots = far.shape[0]
    part = slots // GROUPS
    owned = rb * 128
    per = n // GROUPS
    me = lax.axis_index("curve")
    panel = t2
    loads = [
        pltpu.make_async_copy(panel_hbm, panel, load_sem.at[0]),
        pltpu.make_async_copy(diag_hbm, diag, load_sem.at[1]),
        pltpu.make_async_copy(super_hbm, sup, load_sem.at[2]),
        pltpu.make_async_copy(far_hbm, far, load_sem.at[3]),
    ]
    for load in loads:
        load.start()
    barrier = pltpu.get_barrier_semaphore()

    @pl.loop(1, n)
    def _(k):
        pl.semaphore_signal(barrier, inc=1, device_id=((me + k) % n,), device_id_type=MESH)

    arrive, reductions = rest[: 4 * GROUPS], rest[4 * GROUPS :]
    came1, back1, came2, back2 = (arrive[i * GROUPS : (i + 1) * GROUPS] for i in range(4))
    first_sum, mid_sum, last_sum = (Reduction(reductions[i : i + 6]) for i in (0, 6, 12))
    following, previous = (me + 1) % n, (me + n - 1) % n

    loads[0].wait()
    hi, lo = halves(panel[...])
    cross = nt(hi, lo)
    gram = nt(hi, hi) + (cross + cross.T)
    deg[...] = jnp.zeros_like(deg)
    ones = jnp.ones((16, 128), bf16)

    def column_sums(blk):
        return jnp.sum(blk, axis=0, keepdims=True)

    def near_degree(b4, carry):
        totals = []
        for i in range(4):
            b = b4 * 4 + i
            total = diag[b].astype(f32)
            deg[pl.ds(b, 1), :] += column_sums(total)
            for h in range(bands):
                blk = sup[b, h].astype(f32)
                deg[pl.ds(b + h + 1, 1), :] += column_sums(blk)
                total = total + blk
            totals.append(total)
        high, low = halves(jnp.concatenate(totals, axis=0))
        rows = (nt(ones, high) + nt(ones, low))[0:1]
        for i in range(4):
            deg[pl.ds(b4 * 4 + i, 1), :] += rows[:, i * 128 : i * 128 + 128]
        return carry

    loads[1].wait()
    loads[2].wait()
    lax.fori_loop(0, rb // 4, near_degree, 0)
    pl.semaphore_wait(barrier, n - 1)
    first_sum.start(jnp.concatenate([gram, jnp.zeros_like(gram)], axis=1))
    deg_sent = send(deg.at[pl.ds(rb, 8)], deg_tail, small_sem.at[0], small_sem.at[1], following)
    loads[3].wait()

    def far_pair(k2, sent=(0, 1)):
        to = [partner(2 * k2), partner(2 * k2 + 1)]
        at = [2 * t + c for t in to for c in range(2)]
        blocks = [far[f] for f in at]
        rows = nt(ones, jnp.concatenate(blocks, axis=0))[0:1]
        for i, f in enumerate(at):
            far_sums[pl.ds(f, 1), :] = rows[:, i * 128 : i * 128 + 128]
            cols[f] = column_sums(blocks[i].astype(f32))
        for i in sent:
            send(
                cols.at[pl.ds(2 * to[i], 2)], cols_in.at[pl.ds(2 * me, 2)], small_sem.at[2], small_sem.at[3], to[i]
            )

    def far_step(k2, carry):
        far_pair(k2)
        return carry

    far_pair(0, (1,))
    cols_in[pl.ds(2 * me, 2)] = cols[pl.ds(2 * me, 2)]
    third = n // 6
    lax.fori_loop(1, third + 1, far_step, 0, unroll=3)
    first_sum.across()
    lax.fori_loop(third + 1, 2 * third + 1, far_step, 0, unroll=3)
    first_sum.gather()
    lax.fori_loop(2 * third + 1, n // 2, far_step, 0, unroll=3)

    gram = first_sum.result()[:, :width] * (1.0 / points)
    inverse = chol_inverse(gram)
    h00 = mul_t(mul(inverse, gram), inverse)
    x0[...] = nn3(inverse, panel[...])
    saves = [pltpu.make_async_copy(x0, x_hbm, out_sem.at[0])]
    saves[0].start()

    owner_rows = lax.broadcasted_iota(i32, (rb, slots), 0)
    degree = deg[0:rb, :] + nn((owner_rows == index_v[6:7, :]).astype(f32), far_sums[...], HIGH)
    deg_sent.wait_recv()
    degree = degree + jnp.concatenate([deg_tail[...], jnp.zeros((rb - 8, 128), f32)], axis=0)
    slot_rows = lax.broadcasted_iota(i32, (rb, slots), 0)
    chosen = (slot_rows == index_v[8:9, :]).astype(f32)
    drain(cols_in.at[pl.ds(0, slots - 2)], small_sem.at[3])

    def unpack(f, carry):
        far_sums[pl.ds(f, 1), :] = cols_in[f]
        return carry

    lax.fori_loop(0, slots, unpack, 0, unroll=8)
    degree = degree + nn(chosen, far_sums[...], HIGH)
    root[...] = lax.rsqrt(degree)

    def scale(b, carry):
        v[b] = (x0[:, block(b)] * root[pl.ds(b, 1), :]).astype(bf16)
        return carry

    lax.fori_loop(0, rb, scale, 0, unroll=2)

    zero = jnp.zeros((width, 128), f32)

    def apply(turn, v, came, back, hooks, done):
        ss = [send_sem.at[4 * turn + i] for i in range(4)]
        rs = [recv_sem.at[10 * turn + i] for i in range(10)]
        halo = send(v.at[pl.ds(0, bands)], ahead.at[turn], ss[2], rs[8], previous)

        def stage_one(k):
            t = partner(k)
            for c in range(2):
                stage[2 * t + c] = v[index[0, 2 * t + c]]
            return t

        def mirror_one(k):
            t = partner(k)
            for c in range(2):
                f = 2 * t + c
                mirror[f] = nn(v[index[1, f]], far[f]).astype(bf16)
            return t

        def send_groups(make, src, dst, ssem, rsems, groups):
            if 0 in groups:
                make(0)
                dst[0][0:2] = src[pl.ds(2 * me, 2)]
            for g in groups:

                def step(k, carry, g=g):
                    t = make(k)
                    send(src.at[pl.ds(2 * t, 2)], dst[g].at[pl.ds(2 * (k - g * per), 2)], ssem, rsems[g], t)
                    return carry

                lax.fori_loop(max(1, g * per), (g + 1) * per, step, 0)

        hooks[0]()
        send_groups(stage_one, stage, came, ss[0], rs[0:4], range(GROUPS))
        hooks[1]()
        send_groups(mirror_one, mirror, back, ss[1], rs[4:8], range(GROUPS // 2))

        near[...] = jnp.zeros_like(near)

        def near_one(b, fetch):
            vb = v[b]
            out = nt(vb, diag[b]) + nn(vb, diag[b])
            for h in range(bands):
                out = out + nt(fetch(b + h + 1), sup[b, h])
                near[:, block(b + h + 1)] += nn(vb, sup[b, h])
            near[:, block(b)] += out

        def near_step(b, carry):
            near_one(b, lambda at: v[at])
            return carry

        lax.fori_loop(0, rb - bands, near_step, 0)
        halo.wait_recv()
        for b in range(rb - bands, rb):
            near_one(b, lambda at: v[at] if at < rb else ahead[turn, at - rb])
        tail = send(near.at[:, pl.ds(owned, bands * 128)], tails.at[turn], ss[3], rs[9], following)
        hooks[2]()
        send_groups(mirror_one, mirror, back, ss[1], rs[4:8], range(GROUPS // 2, GROUPS))

        def arrived(ref, g, sem):
            drain(ref[g].at[pl.ds(0, part - 2 if g == 0 else part)], sem)

        for g in range(GROUPS):
            arrived(came, g, rs[g])

            def forward(i4, total, g=g):
                for i in range(4):
                    i1 = i4 * 4 + i
                    j = g * part + i1
                    total = total * keep[0, j] + nt(came[g][index[2, j]], far[index[7, j]])
                    seg[i1] = total
                return total

            lax.fori_loop(0, part // 4, forward, zero)

            def add_forward(b, carry, g=g):
                near[:, block(b)] += seg[index[4, g * rb + b]] * keep[2, g * rb + b]
                return carry

            lax.fori_loop(0, rb, add_forward, 0)
        tail.wait_recv()
        near[:, 0 : bands * 128] += tails[turn]
        hooks[3]()
        for g in range(GROUPS):
            arrived(back, g, rs[4 + g])

            def backward(i4, total, g=g):
                for i in range(4):
                    i1 = i4 * 4 + i
                    j = g * part + i1
                    total = total * keep[1, j] + back[g][index[3, j]].astype(f32)
                    seg[i1] = total
                return total

            lax.fori_loop(0, part // 4, backward, zero)

            def add_backward(b, carry, g=g):
                total = near[:, block(b)] + seg[index[5, g * rb + b]] * keep[3, g * rb + b]
                if g < GROUPS - 1:
                    near[:, block(b)] = total
                else:
                    done(b, total)
                return carry

            lax.fori_loop(0, rb, add_backward, 0, unroll=4)
        halo.wait_send()
        tail.wait_send()
        drain(stage.at[pl.ds(0, slots - 2)], ss[0])
        drain(mirror.at[pl.ds(0, slots - 2)], ss[1])

    def first_done(b, total):
        d = root[pl.ds(b, 1), :]
        t = total * d
        t1[:, block(b)] = t
        u[b] = (t * d).astype(bf16)

    def last_done(b, total):
        t2[:, block(b)] = total * root[pl.ds(b, 1), :]

    apply(0, v, came1, back1, [lambda: None] * 4, first_done)
    saves.append(pltpu.make_async_copy(t1, t1_hbm, out_sem.at[1]))
    saves[1].start()

    kept = []
    lanes = functools.partial(jnp.concatenate, axis=1)

    def early_gram():
        (xh, xl), (ph, pl_) = halves(x0[...]), halves(t1[...])
        c11 = nt(ph, pl_)
        h01 = nt(xh, ph) + (nt(xh, pl_) + nt(xl, ph))
        mid_sum.start(lanes([h01, nt(ph, ph) + (c11 + c11.T)]))

    def early_step():
        sums = mid_sum.result() * (1.0 / points)
        h01, h11 = sums[:, :width], sums[:, width:]
        kept.extend((h00, h01, h11, *first_step(h00, h01, h11)))

    apply(1, u, came2, back2, [early_gram, mid_sum.across, mid_sum.gather, early_step], last_done)
    saves.append(pltpu.make_async_copy(t2, t2_hbm, out_sem.at[2]))
    saves[2].start()

    (th, tl), (xh, xl), (ph, pl_) = halves(t2[...]), halves(x0[...]), halves(t1[...])
    c22 = nt(th, tl)
    h02 = nt(xh, th) + (nt(xh, tl) + nt(xl, th))
    h12 = nt(ph, th) + (nt(ph, tl) + nt(pl_, th))
    h22 = nt(th, th) + (c22 + c22.T)
    last_sum.start(jnp.concatenate([lanes([h02, h12]), lanes([h22, jnp.zeros_like(h22)])], axis=0))
    last_sum.across()
    last_sum.gather()
    sums = last_sum.result() * (1.0 / points)
    new, change = second_step(*kept, sums[:width, :width], sums[:width, width:], sums[width:, :width])
    coef[...] = jnp.zeros_like(coef)
    for i in range(3):
        coef[0:width, i * width : (i + 1) * width] = new[i]
        coef[width:, i * width : (i + 1) * width] = change[i]
    for save in saves:
        save.wait()
    deg_sent.wait_send()
    drain(cols.at[pl.ds(0, slots - 2)], small_sem.at[2])
    first_sum.close()
    mid_sum.close()
    last_sum.close()


def whole(n, tables, panel, diag_blocks, super_blocks, far_blocks):
    rb, bs = diag_blocks.shape[:2]
    bands, slots = super_blocks.shape[1], far_blocks.shape[0]
    width, owned = panel.shape
    index, keep = tables
    here = pl.BlockSpec(memory_space=pltpu.VMEM)
    away = pl.BlockSpec(memory_space=pl.ANY)
    scalar = pl.BlockSpec(memory_space=pltpu.SMEM)
    wide = jax.ShapeDtypeStruct((width, owned), f32)
    blocks = VMEM((slots, width, bs), bf16)
    return pl.pallas_call(
        functools.partial(whole_kernel, n, rb, bands, float(n * owned)),
        out_shape=(wide, wide, wide, jax.ShapeDtypeStruct((2 * width, 4 * width), f32)),
        in_specs=[scalar, scalar, here, away, away, away, away],
        out_specs=(away, away, away, here),
        scratch_shapes=[
            VMEM(diag_blocks.shape, bf16),
            VMEM(super_blocks.shape, bf16),
            VMEM(far_blocks.shape, bf16),
            VMEM((width, owned), f32),
            VMEM((width, owned), f32),
            VMEM((width, owned), f32),
            VMEM((rb, width, bs), bf16),
            VMEM((rb, width, bs), bf16),
            VMEM((rb, bs), f32),
            VMEM((2, bands, width, bs), bf16),
            VMEM((width, owned + bands * bs), f32),
            *[blocks] * 2,
            VMEM((slots // GROUPS, width, bs), f32),
            VMEM((2, width, bands * bs), f32),
            VMEM((rb + 8, bs), f32),
            VMEM((slots, bs), f32),
            VMEM((slots, 1, bs), f32),
            VMEM((slots, 1, bs), f32),
            VMEM((8, bs), f32),
            DMA((4,)),
            DMA((3,)),
            DMA((4,)),
            DMA((8,)),
            DMA((20,)),
            *[VMEM((slots // GROUPS, width, bs), bf16)] * (4 * GROUPS),
            *Reduction.scratch(width),
            *Reduction.scratch(width),
            *Reduction.scratch(2 * width),
        ],
        compiler_params=pltpu.CompilerParams(collective_id=1, has_side_effects=True, vmem_limit_bytes=VM_LIMIT),
        name="whole",
    )(index, keep, index, panel, diag_blocks, super_blocks, far_blocks)


def combine_kernel(coef, x0, t1, t2, basis, update):
    w = x0.shape[0]
    out = nn3(coef[:, 0 : 3 * w], jnp.concatenate([x0[...], t1[...], t2[...]], axis=0))
    basis[...] = out[:w]
    update[...] = out[w:]


def combine(coef, x0, t1, t2):
    w, owned = x0.shape
    chunk = 4096
    panel = pl.BlockSpec((w, chunk), lambda i: (0, i))
    return pl.pallas_call(
        combine_kernel,
        grid=(owned // chunk,),
        out_shape=(jax.ShapeDtypeStruct((w, owned), f32),) * 2,
        in_specs=[pl.BlockSpec(coef.shape, lambda i: (0, 0)), panel, panel, panel],
        out_specs=(panel, panel),
        compiler_params=pltpu.CompilerParams(vmem_limit_bytes=VM_LIMIT),
        name="combine",
    )(coef, x0, t1, t2)


def tables_kernel(n, rb, far_row, send_slot, index, keep):
    slots = far_row.shape[1]
    part = slots // GROUPS
    _, y, x, z, c = position()
    lane = lax.broadcasted_iota(i32, (1, slots), 1)
    other = lane // 2
    dz = (z - (other // 2) % 4 + 4) % 4
    group = (y - other // 32 - dz + 8) % 4
    place = (((x - (other // 8) % 4 - dz + 8) % 4) * 8 + dz * 2 + (c + other) % 2) * 2 + lane % 2
    rows, lanes = (lax.broadcasted_iota(i32, (slots, slots), d) for d in (0, 1))
    same = rows == lanes
    send, far = send_slot[...], far_row[...]
    index[...] = jnp.zeros_like(index)
    keep[...] = jnp.zeros_like(keep)
    index[0:1] = jnp.maximum(send, 0)
    index[1:2] = jnp.maximum(far, 0)
    index[6:7] = far
    index[8:9] = send
    places = jnp.sum(jnp.where(same, jnp.broadcast_to(place, same.shape), 0), axis=1, keepdims=True)
    stride = rb + 2
    target = (lane // rb) * stride + lane % rb + 1
    for at, key in ((0, far), (1, send)):
        kind = group * stride + key + 1
        mixed = kind * slots + lane
        column = jnp.sum(jnp.where(same, jnp.broadcast_to(mixed, same.shape), 0), axis=1, keepdims=True)
        rank = jnp.sum((mixed < column).astype(i32), axis=1, keepdims=True)
        hit = rank == lanes
        ranked = jnp.sum(jnp.where(hit, jnp.broadcast_to(column, hit.shape), 0), axis=0, keepdims=True)
        order = jnp.sum(jnp.where(hit, jnp.broadcast_to(places, hit.shape), 0), axis=0, keepdims=True)
        if at == 0:
            index[7:8] = ranked % slots
        ranked = ranked // slots
        before = jnp.concatenate([jnp.full((1, 1), -1, i32), ranked[:, :-1]], axis=1)
        kinds = column // slots
        last = jnp.sum((kinds <= target).astype(i32), axis=0, keepdims=True) - 1
        found = jnp.sum((kinds == target).astype(i32), axis=0, keepdims=True)
        index[2 + at : 3 + at] = order
        index[4 + at : 5 + at] = jnp.clip(last - (lane // rb) * part, 0, part - 1)
        keep[at : at + 1] = jnp.where(lane % part == 0, 0.0, (ranked == before).astype(f32))
        keep[2 + at : 3 + at] = (found > 0).astype(f32)


def tables_of(n, rb, far_row, send_slot):
    slots = far_row.shape[0]
    here = pl.BlockSpec(memory_space=pltpu.VMEM)
    return pl.pallas_call(
        functools.partial(tables_kernel, n, rb),
        out_shape=(
            jax.ShapeDtypeStruct((16, slots), i32),
            jax.ShapeDtypeStruct((8, slots), f32),
        ),
        in_specs=[here, here],
        out_specs=(here, here),
        name="tables",
    )(far_row.reshape(1, slots), send_slot.reshape(1, slots))


def shards(diag_blocks, super_blocks, far_blocks, far_row, send_slot, panel):
    n = lax.axis_size("curve")
    tables = tables_of(n, diag_blocks.shape[0], far_row, send_slot)
    x0, t1, t2, coef = whole(n, tables, panel, diag_blocks, super_blocks, far_blocks)
    return combine(coef, x0, t1, t2)


def solution(mesh):
    return jax.shard_map(
        shards,
        mesh=mesh,
        in_specs=(
            P("curve", None, None),
            P("curve", None, None, None),
            P("curve", None, None),
            P("curve"),
            P("curve"),
            P(None, "curve"),
        ),
        out_specs=(P(None, "curve"), P(None, "curve")),
        check_vma=False,
    )
```

```python
import functools

import jax
import jax.numpy as jnp
from jax import lax
from jax.experimental import pallas as pl
from jax.experimental.pallas import tpu as pltpu
from jax.sharding import PartitionSpec as P

f32, bf16, i32 = jnp.float32, jnp.bfloat16, jnp.int32
HIGH = lax.Precision.HIGHEST
STEP = 10.0
MOMENTUM = 0.5
MESH = pl.DeviceIdType.MESH
VMEM = pltpu.VMEM
DMA = pltpu.SemaphoreType.DMA
VM_LIMIT = 62 * 2**20


def nn(a, b, precision=None):
    return lax.dot_general(a, b, (((1,), (0,)), ((), ())), precision=precision, preferred_element_type=f32)


def nt(a, b, precision=None):
    return lax.dot_general(a, b, (((1,), (1,)), ((), ())), precision=precision, preferred_element_type=f32)


def halves(x):
    hi = x.astype(bf16)
    return hi, (x - hi.astype(f32)).astype(bf16)


def nn3(a, b):
    (ah, al), (bh, bl) = halves(a), halves(b)
    return nn(jnp.concatenate([ah, ah, al], axis=1), jnp.concatenate([bh, bl, bh], axis=0))


def eye(n, m=None):
    m = m or n
    rows = lax.broadcasted_iota(i32, (n, m), 0)
    return (rows == lax.broadcasted_iota(i32, (n, m), 1)).astype(f32)


def chol_inverse(cross):
    n = cross.shape[0]
    rows, lanes = (lax.broadcasted_iota(i32, (n, n), d) for d in (0, 1))
    diagonal = jnp.where(rows == lanes, cross, 0.0)
    down = lax.rsqrt(jnp.sum(diagonal, axis=1, keepdims=True))
    along = lax.rsqrt(jnp.sum(diagonal, axis=0, keepdims=True))
    both = jnp.concatenate([cross * down * along, eye(n)], axis=1)
    tiles = [both[8 * i : 8 * i + 8] for i in range(n // 8)]
    row_id = lax.broadcasted_iota(i32, (8, 1), 0)
    for k in range(0, n, 2):
        at, sub = k // 8, k % 8
        r0, r1 = tiles[at][sub : sub + 1], tiles[at][sub + 1 : sub + 2]
        a, b, d = r0[:, k : k + 1], r0[:, k + 1 : k + 2], r1[:, k + 1 : k + 2]
        scale = 1.0 / (a * d - b * b)
        p0, p1 = (d * r0 - b * r1) * scale, (a * r1 - b * r0) * scale
        for i in range(at, n // 8):
            if i == at and sub == 6:
                continue
            c0, c1 = tiles[i][:, k : k + 1], tiles[i][:, k + 1 : k + 2]
            if i == at:
                c0, c1 = (jnp.where(row_id > sub + 1, c, 0.0) for c in (c0, c1))
            tiles[i] = tiles[i] - (c0 * p0 + c1 * p1)
    both = jnp.concatenate(tiles, axis=0)
    left, right = both[:, :n], both[:, n:]
    odd = lax.broadcasted_iota(i32, (n, 1), 0) % 2 == 1
    own = jnp.sum(jnp.where(rows == lanes, left, 0.0), axis=1, keepdims=True)
    side = jnp.sum(jnp.where(rows == lanes + 1, left, 0.0), axis=1, keepdims=True)
    above = jnp.concatenate([own[:1], own[:-1]], axis=0)
    ratio = jnp.where(odd, side / above, 0.0)
    upper = jnp.concatenate([right[:1], right[:-1]], axis=0)
    return (right - ratio * upper) * lax.rsqrt(own - ratio * side) * along


def position():
    me = lax.axis_index("curve")
    return me, me // 32, (me // 8) % 4, (me // 2) % 4, me % 2


def partner(k):
    me, y, x, z, c = position()
    dz = (k // 2) % 4
    y, x, z, c = (y + k // 32 + dz) % 4, (x + k // 8 + dz) % 4, (z + dz) % 4, (c + k) % 2
    return ((y * 4 + x) * 4 + z) * 2 + c


def send(src, dst, ssem, rsem, to):
    copy = pltpu.make_async_remote_copy(
        src_ref=src, dst_ref=dst, send_sem=ssem, recv_sem=rsem, device_id=(to,), device_id_type=MESH
    )
    copy.start()
    return copy


def drain(ref, sem):
    pltpu.make_async_copy(ref, ref, sem).wait()


class Reduction:
    @staticmethod
    def scratch(rows):
        piece = rows // 8
        return [
            VMEM((8, piece, 128), f32),
            VMEM((8, piece, 128), f32),
            VMEM((16, piece, 128), f32),
            VMEM((8, piece, 128), f32),
            DMA((3,)),
            DMA((3,)),
        ]

    def __init__(self, refs):
        self.src, self.first, self.second, self.out, self.ss, self.rs = refs
        me = lax.axis_index("curve")
        self.sub = me % 8
        self.plane = me // 8

    def start(self, value):
        piece = value.shape[0] // 8
        for i in range(8):
            self.src[i] = value[i * piece : (i + 1) * piece]
        for k in range(1, 8):
            other = (self.sub + k) % 8
            send(self.src.at[other], self.first.at[self.sub], self.ss.at[0], self.rs.at[0], self.plane * 8 + other)
        self.first[self.sub] = self.src[self.sub]

    def across(self):
        drain(self.first.at[pl.ds(0, 7)], self.rs.at[0])
        total = self.first[0]
        for i in range(1, 8):
            total = total + self.first[i]
        self.second[self.plane] = total
        for k in range(1, 16):
            to = (self.plane + k) % 16 * 8 + self.sub
            send(self.second.at[self.plane], self.second.at[self.plane], self.ss.at[1], self.rs.at[1], to)

    def gather(self):
        drain(self.second.at[pl.ds(0, 15)], self.rs.at[1])
        parts = [self.second[i] for i in range(16)]
        while len(parts) > 1:
            parts = [a + b for a, b in zip(parts[::2], parts[1::2])]
        self.out[self.sub] = parts[0]
        for k in range(1, 8):
            to = self.plane * 8 + (self.sub + k) % 8
            send(self.out.at[self.sub], self.out.at[self.sub], self.ss.at[2], self.rs.at[2], to)

    def result(self):
        drain(self.out.at[pl.ds(0, 7)], self.rs.at[2])
        return jnp.concatenate([self.out[i] for i in range(8)], axis=0)

    def close(self):
        drain(self.src.at[pl.ds(0, 7)], self.ss.at[0])
        drain(self.second.at[pl.ds(0, 15)], self.ss.at[1])
        drain(self.out.at[pl.ds(0, 7)], self.ss.at[2])


def block(b):
    return pl.ds(pl.multiple_of(b * 128, 128), 128)


GROUPS = 4


mul = functools.partial(nn, precision=HIGH)
mul_t = functools.partial(nt, precision=HIGH)


def first_step(h00, h01, h11):
    y0 = eye(h00.shape[0]) - STEP * h01.T
    part = mul(y0, h01)
    m1 = chol_inverse(mul_t(mul(y0, h00), y0) + STEP * (part + part.T) + STEP * STEP * h11)
    return mul(m1, y0), STEP * m1


def second_step(h00, h01, h11, a0, a1, h02, h12, h22):
    one = eye(h00.shape[0])
    s01 = mul_t(h01, a0) + mul_t(h02, a1)
    s11 = mul_t(h11, a0) + mul_t(h12, a1)
    rayleigh = mul(a0, s01) + mul(a1, s11)
    turn = one - STEP * rayleigh.T
    b0 = mul(turn, a0) + MOMENTUM * (a0 - one)
    b1 = mul(turn, a1) + STEP * a0 + MOMENTUM * a1
    b2 = STEP * a1
    p01, p02, p12 = mul(b0, mul_t(h01, b1)), mul(b0, mul_t(h02, b2)), mul(b1, mul_t(h12, b2))
    mixed = p01 + p02 + p12
    square = mul(b0, mul_t(h00, b0)) + mul(b1, mul_t(h11, b1)) + mul(b2, mul_t(h22, b2))
    m2 = chol_inverse(square + (mixed + mixed.T))
    c0, c1, c2 = mul(m2, b0), mul(m2, b1), mul(m2, b2)
    return (c0, c1, c2), (c0 - a0, c1 - a1, c2)


def whole_kernel(
    n, rb, bands, points,
    index, keep, index_v, panel_hbm, diag_hbm, super_hbm, far_hbm,
    x_hbm, t1_hbm, t2_hbm, coef,
    diag, sup, far, x0, t1, t2, v, u, root, ahead, near, stage, mirror, seg, tails,
    deg, far_sums, cols, cols_in, deg_tail, load_sem, out_sem, small_sem, send_sem, recv_sem, *rest,
):
    width = x0.shape[0]
    slots = far.shape[0]
    part = slots // GROUPS
    owned = rb * 128
    per = n // GROUPS
    me = lax.axis_index("curve")
    panel = t2
    loads = [
        pltpu.make_async_copy(panel_hbm, panel, load_sem.at[0]),
        pltpu.make_async_copy(diag_hbm, diag, load_sem.at[1]),
        pltpu.make_async_copy(super_hbm, sup, load_sem.at[2]),
        pltpu.make_async_copy(far_hbm, far, load_sem.at[3]),
    ]
    for load in loads:
        load.start()
    barrier = pltpu.get_barrier_semaphore()

    greetings = 4 * n // rb

    def greet(k):
        pl.semaphore_signal(barrier, inc=1, device_id=((me + k) % n,), device_id_type=MESH)

    arrive, reductions = rest[: 4 * GROUPS], rest[4 * GROUPS :]
    came1, back1, came2, back2 = (arrive[i * GROUPS : (i + 1) * GROUPS] for i in range(4))
    first_sum, mid_sum, last_sum = (Reduction(reductions[i : i + 6]) for i in (0, 6, 12))
    following, previous = (me + 1) % n, (me + n - 1) % n

    loads[0].wait()
    hi, lo = halves(panel[...])
    cross = nt(hi, lo)
    gram = nt(hi, hi) + (cross + cross.T)
    deg[...] = jnp.zeros_like(deg)
    ones = jnp.ones((16, 128), bf16)

    def column_sums(blk):
        return jnp.sum(blk, axis=0, keepdims=True)

    def near_degree(b4, carry):
        for i in range(1, greetings):
            greet(b4 * greetings + i)

        @pl.when(b4 > 0)
        def _():
            greet(b4 * greetings)

        totals = []
        for i in range(4):
            b = b4 * 4 + i
            total = diag[b].astype(f32)
            deg[pl.ds(b, 1), :] += column_sums(total)
            for h in range(bands):
                blk = sup[b, h].astype(f32)
                deg[pl.ds(b + h + 1, 1), :] += column_sums(blk)
                total = total + blk
            totals.append(total)
        high, low = halves(jnp.concatenate(totals, axis=0))
        rows = (nt(ones, high) + nt(ones, low))[0:1]
        for i in range(4):
            deg[pl.ds(b4 * 4 + i, 1), :] += rows[:, i * 128 : i * 128 + 128]
        return carry

    loads[1].wait()
    loads[2].wait()
    lax.fori_loop(0, rb // 4, near_degree, 0)
    pl.semaphore_wait(barrier, n - 1)
    first_sum.start(jnp.concatenate([gram, jnp.zeros_like(gram)], axis=1))
    deg_sent = send(deg.at[pl.ds(rb, 8)], deg_tail, small_sem.at[0], small_sem.at[1], following)
    loads[3].wait()

    def far_pair(k2, sent=(0, 1)):
        to = [partner(2 * k2), partner(2 * k2 + 1)]
        at = [2 * t + c for t in to for c in range(2)]
        blocks = [far[f] for f in at]
        rows = nt(ones, jnp.concatenate(blocks, axis=0))[0:1]
        for i, f in enumerate(at):
            far_sums[pl.ds(f, 1), :] = rows[:, i * 128 : i * 128 + 128]
            cols[f] = column_sums(blocks[i].astype(f32))
        for i in sent:
            send(
                cols.at[pl.ds(2 * to[i], 2)], cols_in.at[pl.ds(2 * me, 2)], small_sem.at[2], small_sem.at[3], to[i]
            )

    def far_step(k2, carry):
        far_pair(k2)
        return carry

    far_pair(0, (1,))
    cols_in[pl.ds(2 * me, 2)] = cols[pl.ds(2 * me, 2)]
    third = n // 6
    lax.fori_loop(1, third + 1, far_step, 0, unroll=3)
    first_sum.across()
    lax.fori_loop(third + 1, 2 * third + 1, far_step, 0, unroll=3)
    first_sum.gather()
    lax.fori_loop(2 * third + 1, n // 2, far_step, 0, unroll=3)

    gram = first_sum.result()[:, :width] * (1.0 / points)
    inverse = chol_inverse(gram)
    h00 = mul_t(mul(inverse, gram), inverse)
    x0[...] = nn3(inverse, panel[...])
    saves = [pltpu.make_async_copy(x0, x_hbm, out_sem.at[0])]
    saves[0].start()

    owner_rows = lax.broadcasted_iota(i32, (rb, slots), 0)
    degree = deg[0:rb, :] + nn((owner_rows == index_v[6:7, :]).astype(f32), far_sums[...], HIGH)
    deg_sent.wait_recv()
    degree = degree + jnp.concatenate([deg_tail[...], jnp.zeros((rb - 8, 128), f32)], axis=0)
    slot_rows = lax.broadcasted_iota(i32, (rb, slots), 0)
    chosen = (slot_rows == index_v[8:9, :]).astype(f32)
    drain(cols_in.at[pl.ds(0, slots - 2)], small_sem.at[3])

    def unpack(f, carry):
        far_sums[pl.ds(f, 1), :] = cols_in[f]
        return carry

    lax.fori_loop(0, slots, unpack, 0, unroll=8)
    degree = degree + nn(chosen, far_sums[...], HIGH)
    root[...] = lax.rsqrt(degree)

    def scale(b, carry):
        v[b] = (x0[:, block(b)] * root[pl.ds(b, 1), :]).astype(bf16)
        return carry

    lax.fori_loop(0, rb, scale, 0, unroll=2)

    zero = jnp.zeros((width, 128), f32)

    def apply(turn, v, came, back, hooks, done):
        ss = [send_sem.at[4 * turn + i] for i in range(4)]
        rs = [recv_sem.at[10 * turn + i] for i in range(10)]
        halo = send(v.at[pl.ds(0, bands)], ahead.at[turn], ss[2], rs[8], previous)

        def stage_one(k):
            t = partner(k)
            for c in range(2):
                stage[2 * t + c] = v[index[0, 2 * t + c]]
            return t

        def mirror_one(k):
            t = partner(k)
            for c in range(2):
                f = 2 * t + c
                mirror[f] = nn(v[index[1, f]], far[f]).astype(bf16)
            return t

        def send_groups(make, src, dst, ssem, rsems, groups):
            if 0 in groups:
                make(0)
                dst[0][0:2] = src[pl.ds(2 * me, 2)]
            for g in groups:

                def step(k, carry, g=g):
                    t = make(k)
                    send(src.at[pl.ds(2 * t, 2)], dst[g].at[pl.ds(2 * (k - g * per), 2)], ssem, rsems[g], t)
                    return carry

                lax.fori_loop(max(1, g * per), (g + 1) * per, step, 0)

        hooks[0]()
        send_groups(stage_one, stage, came, ss[0], rs[0:4], range(GROUPS))
        hooks[1]()
        send_groups(mirror_one, mirror, back, ss[1], rs[4:8], range(GROUPS // 2))

        near[...] = jnp.zeros_like(near)

        def near_one(b, fetch):
            vb = v[b]
            out = nt(vb, diag[b]) + nn(vb, diag[b])
            for h in range(bands):
                out = out + nt(fetch(b + h + 1), sup[b, h])
                near[:, block(b + h + 1)] += nn(vb, sup[b, h])
            near[:, block(b)] += out

        def near_step(b, carry):
            near_one(b, lambda at: v[at])
            return carry

        lax.fori_loop(0, rb - bands, near_step, 0)
        halo.wait_recv()
        for b in range(rb - bands, rb):
            near_one(b, lambda at: v[at] if at < rb else ahead[turn, at - rb])
        tail = send(near.at[:, pl.ds(owned, bands * 128)], tails.at[turn], ss[3], rs[9], following)
        hooks[2]()
        send_groups(mirror_one, mirror, back, ss[1], rs[4:8], range(GROUPS // 2, GROUPS))

        def arrived(ref, g, sem):
            drain(ref[g].at[pl.ds(0, part - 2 if g == 0 else part)], sem)

        for g in range(GROUPS):
            arrived(came, g, rs[g])

            def forward(i4, total, g=g):
                for i in range(4):
                    i1 = i4 * 4 + i
                    j = g * part + i1
                    total = total * keep[0, j] + nt(came[g][index[2, j]], far[index[7, j]])
                    seg[i1] = total
                return total

            lax.fori_loop(0, part // 4, forward, zero)

            def add_forward(b, carry, g=g):
                near[:, block(b)] += seg[index[4, g * rb + b]] * keep[2, g * rb + b]
                return carry

            lax.fori_loop(0, rb, add_forward, 0)
        tail.wait_recv()
        near[:, 0 : bands * 128] += tails[turn]
        hooks[3]()
        for g in range(GROUPS):
            arrived(back, g, rs[4 + g])

            def backward(i4, total, g=g):
                for i in range(4):
                    i1 = i4 * 4 + i
                    j = g * part + i1
                    total = total * keep[1, j] + back[g][index[3, j]].astype(f32)
                    seg[i1] = total
                return total

            lax.fori_loop(0, part // 4, backward, zero)

            def add_backward(b, carry, g=g):
                total = near[:, block(b)] + seg[index[5, g * rb + b]] * keep[3, g * rb + b]
                if g < GROUPS - 1:
                    near[:, block(b)] = total
                else:
                    done(b, total)
                return carry

            lax.fori_loop(0, rb, add_backward, 0, unroll=4)
        halo.wait_send()
        tail.wait_send()
        drain(stage.at[pl.ds(0, slots - 2)], ss[0])
        drain(mirror.at[pl.ds(0, slots - 2)], ss[1])

    def first_done(b, total):
        d = root[pl.ds(b, 1), :]
        t = total * d
        t1[:, block(b)] = t
        u[b] = (t * d).astype(bf16)

    def last_done(b, total):
        t2[:, block(b)] = total * root[pl.ds(b, 1), :]

    apply(0, v, came1, back1, [lambda: None] * 4, first_done)
    saves.append(pltpu.make_async_copy(t1, t1_hbm, out_sem.at[1]))
    saves[1].start()

    kept = []
    lanes = functools.partial(jnp.concatenate, axis=1)

    def early_gram():
        (xh, xl), (ph, pl_) = halves(x0[...]), halves(t1[...])
        c11 = nt(ph, pl_)
        h01 = nt(xh, ph) + (nt(xh, pl_) + nt(xl, ph))
        mid_sum.start(lanes([h01, nt(ph, ph) + (c11 + c11.T)]))

    def early_step():
        sums = mid_sum.result() * (1.0 / points)
        h01, h11 = sums[:, :width], sums[:, width:]
        kept.extend((h00, h01, h11, *first_step(h00, h01, h11)))

    apply(1, u, came2, back2, [early_gram, mid_sum.across, mid_sum.gather, early_step], last_done)
    saves.append(pltpu.make_async_copy(t2, t2_hbm, out_sem.at[2]))
    saves[2].start()

    (th, tl), (xh, xl), (ph, pl_) = halves(t2[...]), halves(x0[...]), halves(t1[...])
    by_high = nt(jnp.concatenate([xh, ph, th], axis=0), th)
    low_by_high = nt(jnp.concatenate([xl, pl_, tl], axis=0), th)
    by_low = nt(jnp.concatenate([xh, ph], axis=0), tl)
    c22 = low_by_high[2 * width :]
    both = by_high[: 2 * width] + (by_low + low_by_high[: 2 * width])
    h02, h12 = both[:width], both[width:]
    h22 = by_high[2 * width :] + (c22 + c22.T)
    last_sum.start(jnp.concatenate([lanes([h02, h12]), lanes([h22, jnp.zeros_like(h22)])], axis=0))
    last_sum.across()
    last_sum.gather()
    sums = last_sum.result() * (1.0 / points)
    new, change = second_step(*kept, sums[:width, :width], sums[:width, width:], sums[width:, :width])
    coef[...] = jnp.zeros_like(coef)
    for i in range(3):
        coef[0:width, i * width : (i + 1) * width] = new[i]
        coef[width:, i * width : (i + 1) * width] = change[i]
    for save in saves:
        save.wait()
    deg_sent.wait_send()
    drain(cols.at[pl.ds(0, slots - 2)], small_sem.at[2])
    first_sum.close()
    mid_sum.close()
    last_sum.close()


def whole(n, tables, panel, diag_blocks, super_blocks, far_blocks):
    rb, bs = diag_blocks.shape[:2]
    bands, slots = super_blocks.shape[1], far_blocks.shape[0]
    width, owned = panel.shape
    index, keep = tables
    here = pl.BlockSpec(memory_space=pltpu.VMEM)
    away = pl.BlockSpec(memory_space=pl.ANY)
    scalar = pl.BlockSpec(memory_space=pltpu.SMEM)
    wide = jax.ShapeDtypeStruct((width, owned), f32)
    blocks = VMEM((slots, width, bs), bf16)
    return pl.pallas_call(
        functools.partial(whole_kernel, n, rb, bands, float(n * owned)),
        out_shape=(wide, wide, wide, jax.ShapeDtypeStruct((2 * width, 4 * width), f32)),
        in_specs=[scalar, scalar, here, away, away, away, away],
        out_specs=(away, away, away, here),
        scratch_shapes=[
            VMEM(diag_blocks.shape, bf16),
            VMEM(super_blocks.shape, bf16),
            VMEM(far_blocks.shape, bf16),
            VMEM((width, owned), f32),
            VMEM((width, owned), f32),
            VMEM((width, owned), f32),
            VMEM((rb, width, bs), bf16),
            VMEM((rb, width, bs), bf16),
            VMEM((rb, bs), f32),
            VMEM((2, bands, width, bs), bf16),
            VMEM((width, owned + bands * bs), f32),
            *[blocks] * 2,
            VMEM((slots // GROUPS, width, bs), f32),
            VMEM((2, width, bands * bs), f32),
            VMEM((rb + 8, bs), f32),
            VMEM((slots, bs), f32),
            VMEM((slots, 1, bs), f32),
            VMEM((slots, 1, bs), f32),
            VMEM((8, bs), f32),
            DMA((4,)),
            DMA((3,)),
            DMA((4,)),
            DMA((8,)),
            DMA((20,)),
            *[VMEM((slots // GROUPS, width, bs), bf16)] * (4 * GROUPS),
            *Reduction.scratch(width),
            *Reduction.scratch(width),
            *Reduction.scratch(2 * width),
        ],
        compiler_params=pltpu.CompilerParams(collective_id=1, has_side_effects=True, vmem_limit_bytes=VM_LIMIT),
        name="whole",
    )(index, keep, index, panel, diag_blocks, super_blocks, far_blocks)


def combine_kernel(coef, x0, t1, t2, basis, update):
    w = x0.shape[0]
    out = nn3(coef[:, 0 : 3 * w], jnp.concatenate([x0[...], t1[...], t2[...]], axis=0))
    basis[...] = out[:w]
    update[...] = out[w:]


def combine(coef, x0, t1, t2):
    w, owned = x0.shape
    chunk = 4096
    panel = pl.BlockSpec((w, chunk), lambda i: (0, i))
    return pl.pallas_call(
        combine_kernel,
        grid=(owned // chunk,),
        out_shape=(jax.ShapeDtypeStruct((w, owned), f32),) * 2,
        in_specs=[pl.BlockSpec(coef.shape, lambda i: (0, 0)), panel, panel, panel],
        out_specs=(panel, panel),
        compiler_params=pltpu.CompilerParams(vmem_limit_bytes=VM_LIMIT),
        name="combine",
    )(coef, x0, t1, t2)


def tables_kernel(n, rb, far_row, send_slot, index, keep):
    slots = far_row.shape[1]
    part = slots // GROUPS
    _, y, x, z, c = position()
    lane = lax.broadcasted_iota(i32, (1, slots), 1)
    other = lane // 2
    dz = (z - (other // 2) % 4 + 4) % 4
    group = (y - other // 32 - dz + 8) % 4
    place = (((x - (other // 8) % 4 - dz + 8) % 4) * 8 + dz * 2 + (c + other) % 2) * 2 + lane % 2
    rows, lanes = (lax.broadcasted_iota(i32, (slots, slots), d) for d in (0, 1))
    same = rows == lanes
    send, far = send_slot[...], far_row[...]
    index[...] = jnp.zeros_like(index)
    keep[...] = jnp.zeros_like(keep)
    index[0:1] = jnp.maximum(send, 0)
    index[1:2] = jnp.maximum(far, 0)
    index[6:7] = far
    index[8:9] = send
    places = jnp.sum(jnp.where(same, jnp.broadcast_to(place, same.shape), 0), axis=1, keepdims=True)
    stride = rb + 2
    target = (lane // rb) * stride + lane % rb + 1
    for at, key in ((0, far), (1, send)):
        kind = group * stride + key + 1
        mixed = kind * slots + lane
        column = jnp.sum(jnp.where(same, jnp.broadcast_to(mixed, same.shape), 0), axis=1, keepdims=True)
        rank = jnp.sum((mixed < column).astype(i32), axis=1, keepdims=True)
        hit = rank == lanes
        ranked = jnp.sum(jnp.where(hit, jnp.broadcast_to(column, hit.shape), 0), axis=0, keepdims=True)
        order = jnp.sum(jnp.where(hit, jnp.broadcast_to(places, hit.shape), 0), axis=0, keepdims=True)
        if at == 0:
            index[7:8] = ranked % slots
        ranked = ranked // slots
        before = jnp.concatenate([jnp.full((1, 1), -1, i32), ranked[:, :-1]], axis=1)
        kinds = column // slots
        last = jnp.sum((kinds <= target).astype(i32), axis=0, keepdims=True) - 1
        found = jnp.sum((kinds == target).astype(i32), axis=0, keepdims=True)
        index[2 + at : 3 + at] = order
        index[4 + at : 5 + at] = jnp.clip(last - (lane // rb) * part, 0, part - 1)
        keep[at : at + 1] = jnp.where(lane % part == 0, 0.0, (ranked == before).astype(f32))
        keep[2 + at : 3 + at] = (found > 0).astype(f32)


def tables_of(n, rb, far_row, send_slot):
    slots = far_row.shape[0]
    here = pl.BlockSpec(memory_space=pltpu.VMEM)
    return pl.pallas_call(
        functools.partial(tables_kernel, n, rb),
        out_shape=(
            jax.ShapeDtypeStruct((16, slots), i32),
            jax.ShapeDtypeStruct((8, slots), f32),
        ),
        in_specs=[here, here],
        out_specs=(here, here),
        name="tables",
    )(far_row.reshape(1, slots), send_slot.reshape(1, slots))


def shards(diag_blocks, super_blocks, far_blocks, far_row, send_slot, panel):
    n = lax.axis_size("curve")
    tables = tables_of(n, diag_blocks.shape[0], far_row, send_slot)
    x0, t1, t2, coef = whole(n, tables, panel, diag_blocks, super_blocks, far_blocks)
    return combine(coef, x0, t1, t2)


def solution(mesh):
    return jax.shard_map(
        shards,
        mesh=mesh,
        in_specs=(
            P("curve", None, None),
            P("curve", None, None, None),
            P("curve", None, None),
            P("curve"),
            P("curve"),
            P(None, "curve"),
        ),
        out_specs=(P(None, "curve"), P(None, "curve")),
        check_vma=False,
    )
```

```python
import functools

import jax
import jax.numpy as jnp
from jax import lax
from jax.experimental import pallas as pl
from jax.experimental.pallas import tpu as pltpu
from jax.sharding import PartitionSpec as P

f32, bf16, i32 = jnp.float32, jnp.bfloat16, jnp.int32
HIGH = lax.Precision.HIGHEST
STEP = 10.0
MOMENTUM = 0.5
MESH = pl.DeviceIdType.MESH
VMEM = pltpu.VMEM
DMA = pltpu.SemaphoreType.DMA
VM_LIMIT = 62 * 2**20


def nn(a, b, precision=None):
    return lax.dot_general(a, b, (((1,), (0,)), ((), ())), precision=precision, preferred_element_type=f32)


def nt(a, b, precision=None):
    return lax.dot_general(a, b, (((1,), (1,)), ((), ())), precision=precision, preferred_element_type=f32)


def halves(x):
    hi = x.astype(bf16)
    return hi, (x - hi.astype(f32)).astype(bf16)


def nn3(a, b):
    (ah, al), (bh, bl) = halves(a), halves(b)
    return nn(ah, bh) + (nn(ah, bl) + nn(al, bh))


def nt3(a, b):
    (ah, al), (bh, bl) = halves(a), halves(b)
    return nt(ah, bh) + (nt(ah, bl) + nt(al, bh))


def eye(n, m=None):
    m = m or n
    rows = lax.broadcasted_iota(i32, (n, m), 0)
    return (rows == lax.broadcasted_iota(i32, (n, m), 1)).astype(f32)


def chol_inverse(cross):
    n = cross.shape[0]
    rows, lanes = (lax.broadcasted_iota(i32, (n, n), d) for d in (0, 1))
    diagonal = jnp.where(rows == lanes, cross, 0.0)
    down = lax.rsqrt(jnp.sum(diagonal, axis=1, keepdims=True))
    along = lax.rsqrt(jnp.sum(diagonal, axis=0, keepdims=True))
    both = jnp.concatenate([cross * down * along, eye(n)], axis=1)
    tiles = [both[8 * i : 8 * i + 8] for i in range(n // 8)]
    row_id = lax.broadcasted_iota(i32, (8, 1), 0)
    for k in range(0, n, 2):
        at, sub = k // 8, k % 8
        r0, r1 = tiles[at][sub : sub + 1], tiles[at][sub + 1 : sub + 2]
        a, b, d = r0[:, k : k + 1], r0[:, k + 1 : k + 2], r1[:, k + 1 : k + 2]
        scale = 1.0 / (a * d - b * b)
        p0, p1 = (d * r0 - b * r1) * scale, (a * r1 - b * r0) * scale
        for i in range(at, n // 8):
            if i == at and sub == 6:
                continue
            c0, c1 = tiles[i][:, k : k + 1], tiles[i][:, k + 1 : k + 2]
            if i == at:
                c0, c1 = (jnp.where(row_id > sub + 1, c, 0.0) for c in (c0, c1))
            tiles[i] = tiles[i] - (c0 * p0 + c1 * p1)
    both = jnp.concatenate(tiles, axis=0)
    left, right = both[:, :n], both[:, n:]
    odd = lax.broadcasted_iota(i32, (n, 1), 0) % 2 == 1
    own = jnp.sum(jnp.where(rows == lanes, left, 0.0), axis=1, keepdims=True)
    side = jnp.sum(jnp.where(rows == lanes + 1, left, 0.0), axis=1, keepdims=True)
    above = jnp.concatenate([own[:1], own[:-1]], axis=0)
    ratio = jnp.where(odd, side / above, 0.0)
    upper = jnp.concatenate([right[:1], right[:-1]], axis=0)
    return (right - ratio * upper) * lax.rsqrt(own - ratio * side) * along


def position():
    me = lax.axis_index("curve")
    return me, me // 32, (me // 8) % 4, (me // 2) % 4, me % 2


def partner(k):
    me, y, x, z, c = position()
    dz = (k // 2) % 4
    y, x, z, c = (y + k // 32 + dz) % 4, (x + k // 8 + dz) % 4, (z + dz) % 4, (c + k) % 2
    return ((y * 4 + x) * 4 + z) * 2 + c


def send(src, dst, ssem, rsem, to):
    copy = pltpu.make_async_remote_copy(
        src_ref=src, dst_ref=dst, send_sem=ssem, recv_sem=rsem, device_id=(to,), device_id_type=MESH
    )
    copy.start()
    return copy


def drain(ref, sem):
    pltpu.make_async_copy(ref, ref, sem).wait()


class Reduction:
    @staticmethod
    def scratch(rows):
        piece = rows // 8
        return [
            VMEM((8, piece, 128), f32),
            VMEM((8, piece, 128), f32),
            VMEM((16, piece, 128), f32),
            VMEM((8, piece, 128), f32),
            DMA((3,)),
            DMA((3,)),
        ]

    def __init__(self, refs):
        self.src, self.first, self.second, self.out, self.ss, self.rs = refs
        me = lax.axis_index("curve")
        self.sub = me % 8
        self.plane = me // 8

    def start(self, value):
        piece = value.shape[0] // 8
        for i in range(8):
            self.src[i] = value[i * piece : (i + 1) * piece]
        for k in range(1, 8):
            other = (self.sub + k) % 8
            send(self.src.at[other], self.first.at[self.sub], self.ss.at[0], self.rs.at[0], self.plane * 8 + other)
        self.first[self.sub] = self.src[self.sub]

    def across(self):
        drain(self.first.at[pl.ds(0, 7)], self.rs.at[0])
        total = self.first[0]
        for i in range(1, 8):
            total = total + self.first[i]
        self.second[self.plane] = total
        for k in range(1, 16):
            to = (self.plane + k) % 16 * 8 + self.sub
            send(self.second.at[self.plane], self.second.at[self.plane], self.ss.at[1], self.rs.at[1], to)

    def gather(self):
        drain(self.second.at[pl.ds(0, 15)], self.rs.at[1])
        parts = [self.second[i] for i in range(16)]
        while len(parts) > 1:
            parts = [a + b for a, b in zip(parts[::2], parts[1::2])]
        self.out[self.sub] = parts[0]
        for k in range(1, 8):
            to = self.plane * 8 + (self.sub + k) % 8
            send(self.out.at[self.sub], self.out.at[self.sub], self.ss.at[2], self.rs.at[2], to)

    def result(self):
        drain(self.out.at[pl.ds(0, 7)], self.rs.at[2])
        return jnp.concatenate([self.out[i] for i in range(8)], axis=0)

    def close(self):
        drain(self.src.at[pl.ds(0, 7)], self.ss.at[0])
        drain(self.second.at[pl.ds(0, 15)], self.ss.at[1])
        drain(self.out.at[pl.ds(0, 7)], self.ss.at[2])


def block(b):
    return pl.ds(pl.multiple_of(b * 128, 128), 128)


GROUPS = 4


mul = functools.partial(nn, precision=HIGH)
mul_t = functools.partial(nt, precision=HIGH)


def first_step(h00, h01, h11):
    y0 = eye(h00.shape[0]) - STEP * h01.T
    part = mul(y0, h01)
    m1 = chol_inverse(mul_t(mul(y0, h00), y0) + STEP * (part + part.T) + STEP * STEP * h11)
    return mul(m1, y0), STEP * m1


def second_step(h00, h01, h11, a0, a1, h02, h12, h22):
    one = eye(h00.shape[0])
    s01 = mul_t(h01, a0) + mul_t(h02, a1)
    s11 = mul_t(h11, a0) + mul_t(h12, a1)
    rayleigh = mul(a0, s01) + mul(a1, s11)
    turn = one - STEP * rayleigh.T
    b0 = mul(turn, a0) + MOMENTUM * (a0 - one)
    b1 = mul(turn, a1) + STEP * a0 + MOMENTUM * a1
    b2 = STEP * a1
    p01, p02, p12 = mul(b0, mul_t(h01, b1)), mul(b0, mul_t(h02, b2)), mul(b1, mul_t(h12, b2))
    mixed = p01 + p02 + p12
    square = mul(b0, mul_t(h00, b0)) + mul(b1, mul_t(h11, b1)) + mul(b2, mul_t(h22, b2))
    m2 = chol_inverse(square + (mixed + mixed.T))
    c0, c1, c2 = mul(m2, b0), mul(m2, b1), mul(m2, b2)
    return (c0, c1, c2), (c0 - a0, c1 - a1, c2)


def whole_kernel(
    n, rb, bands, points,
    index, keep, index_v, panel_hbm, diag_hbm, super_hbm, far_hbm,
    x_hbm, t1_hbm, t2_hbm, coef,
    diag, sup, far, x0, t1, t2, v, u, root, ahead, near, stage, mirror, seg, tails,
    deg, far_sums, cols, cols_in, deg_tail, load_sem, out_sem, small_sem, send_sem, recv_sem, *rest,
):
    width = x0.shape[0]
    slots = far.shape[0]
    part = slots // GROUPS
    owned = rb * 128
    per = n // GROUPS
    me = lax.axis_index("curve")
    panel = t2
    loads = [
        pltpu.make_async_copy(panel_hbm, panel, load_sem.at[0]),
        pltpu.make_async_copy(diag_hbm, diag, load_sem.at[1]),
        pltpu.make_async_copy(super_hbm, sup, load_sem.at[2]),
        pltpu.make_async_copy(far_hbm, far, load_sem.at[3]),
    ]
    for load in loads:
        load.start()
    barrier = pltpu.get_barrier_semaphore()

    @pl.loop(1, n)
    def _(k):
        pl.semaphore_signal(barrier, inc=1, device_id=((me + k) % n,), device_id_type=MESH)

    arrive, reductions = rest[: 4 * GROUPS], rest[4 * GROUPS :]
    came1, back1, came2, back2 = (arrive[i * GROUPS : (i + 1) * GROUPS] for i in range(4))
    first_sum, mid_sum, last_sum = (Reduction(reductions[i : i + 6]) for i in (0, 6, 12))
    following, previous = (me + 1) % n, (me + n - 1) % n

    loads[0].wait()
    hi, lo = halves(panel[...])
    cross = nt(hi, lo)
    gram = nt(hi, hi) + (cross + cross.T)
    deg[...] = jnp.zeros_like(deg)
    ones = jnp.ones((16, 128), bf16)

    def column_sums(blk):
        return jnp.sum(blk, axis=0, keepdims=True)

    def near_degree(b4, carry):
        totals = []
        for i in range(4):
            b = b4 * 4 + i
            total = diag[b].astype(f32)
            deg[pl.ds(b, 1), :] += column_sums(total)
            for h in range(bands):
                blk = sup[b, h].astype(f32)
                deg[pl.ds(b + h + 1, 1), :] += column_sums(blk)
                total = total + blk
            totals.append(total)
        high, low = halves(jnp.concatenate(totals, axis=0))
        rows = (nt(ones, high) + nt(ones, low))[0:1]
        for i in range(4):
            deg[pl.ds(b4 * 4 + i, 1), :] += rows[:, i * 128 : i * 128 + 128]
        return carry

    loads[1].wait()
    loads[2].wait()
    lax.fori_loop(0, rb // 4, near_degree, 0)
    pl.semaphore_wait(barrier, n - 1)
    first_sum.start(jnp.concatenate([gram, jnp.zeros_like(gram)], axis=1))
    deg_sent = send(deg.at[pl.ds(rb, 8)], deg_tail, small_sem.at[0], small_sem.at[1], following)
    loads[3].wait()

    def far_pair(k2, sent=(0, 1)):
        to = [partner(2 * k2), partner(2 * k2 + 1)]
        at = [2 * t + c for t in to for c in range(2)]
        blocks = [far[f] for f in at]
        rows = nt(ones, jnp.concatenate(blocks, axis=0))[0:1]
        for i, f in enumerate(at):
            far_sums[pl.ds(f, 1), :] = rows[:, i * 128 : i * 128 + 128]
            cols[f] = column_sums(blocks[i].astype(f32))
        for i in sent:
            send(
                cols.at[pl.ds(2 * to[i], 2)], cols_in.at[pl.ds(2 * me, 2)], small_sem.at[2], small_sem.at[3], to[i]
            )

    def far_step(k2, carry):
        far_pair(k2)
        return carry

    far_pair(0, (1,))
    cols_in[pl.ds(2 * me, 2)] = cols[pl.ds(2 * me, 2)]
    third = n // 6
    lax.fori_loop(1, third + 1, far_step, 0, unroll=3)
    first_sum.across()
    lax.fori_loop(third + 1, 2 * third + 1, far_step, 0, unroll=3)
    first_sum.gather()
    lax.fori_loop(2 * third + 1, n // 2, far_step, 0, unroll=3)

    gram = first_sum.result()[:, :width] * (1.0 / points)
    inverse = chol_inverse(gram)
    h00 = mul_t(mul(inverse, gram), inverse)
    x0[...] = nn3(inverse, panel[...])
    saves = [pltpu.make_async_copy(x0, x_hbm, out_sem.at[0])]
    saves[0].start()

    owner_rows = lax.broadcasted_iota(i32, (rb, slots), 0)
    degree = deg[0:rb, :] + nn((owner_rows == index_v[6:7, :]).astype(f32), far_sums[...], HIGH)
    deg_sent.wait_recv()
    degree = degree + jnp.concatenate([deg_tail[...], jnp.zeros((rb - 8, 128), f32)], axis=0)
    slot_rows = lax.broadcasted_iota(i32, (rb, slots), 0)
    chosen = (slot_rows == index_v[8:9, :]).astype(f32)
    drain(cols_in.at[pl.ds(0, slots - 2)], small_sem.at[3])

    def unpack(f, carry):
        far_sums[pl.ds(f, 1), :] = cols_in[f]
        return carry

    lax.fori_loop(0, slots, unpack, 0, unroll=8)
    degree = degree + nn(chosen, far_sums[...], HIGH)
    root[...] = lax.rsqrt(degree)

    def scale(b, carry):
        v[b] = (x0[:, block(b)] * root[pl.ds(b, 1), :]).astype(bf16)
        return carry

    lax.fori_loop(0, rb, scale, 0, unroll=2)

    zero = jnp.zeros((width, 128), f32)

    def apply(turn, v, came, back, hooks, done):
        ss = [send_sem.at[4 * turn + i] for i in range(4)]
        rs = [recv_sem.at[10 * turn + i] for i in range(10)]
        halo = send(v.at[pl.ds(0, bands)], ahead.at[turn], ss[2], rs[8], previous)

        def stage_one(k):
            t = partner(k)
            for c in range(2):
                stage[2 * t + c] = v[index[0, 2 * t + c]]
            return t

        def mirror_one(k):
            t = partner(k)
            for c in range(2):
                f = 2 * t + c
                mirror[f] = nn(v[index[1, f]], far[f]).astype(bf16)
            return t

        def send_groups(make, src, dst, ssem, rsems, groups):
            if 0 in groups:
                make(0)
                dst[0][0:2] = src[pl.ds(2 * me, 2)]
            for g in groups:

                def step(k, carry, g=g):
                    t = make(k)
                    send(src.at[pl.ds(2 * t, 2)], dst[g].at[pl.ds(2 * (k - g * per), 2)], ssem, rsems[g], t)
                    return carry

                lax.fori_loop(max(1, g * per), (g + 1) * per, step, 0)

        hooks[0]()
        send_groups(stage_one, stage, came, ss[0], rs[0:4], range(GROUPS))
        hooks[1]()
        send_groups(mirror_one, mirror, back, ss[1], rs[4:8], range(GROUPS // 2))

        near[...] = jnp.zeros_like(near)

        def near_one(b, fetch):
            vb = v[b]
            out = nt(vb, diag[b]) + nn(vb, diag[b])
            for h in range(bands):
                out = out + nt(fetch(b + h + 1), sup[b, h])
                near[:, block(b + h + 1)] += nn(vb, sup[b, h])
            near[:, block(b)] += out

        def near_step(b, carry):
            near_one(b, lambda at: v[at])
            return carry

        lax.fori_loop(0, rb - bands, near_step, 0)
        halo.wait_recv()
        for b in range(rb - bands, rb):
            near_one(b, lambda at: v[at] if at < rb else ahead[turn, at - rb])
        tail = send(near.at[:, pl.ds(owned, bands * 128)], tails.at[turn], ss[3], rs[9], following)
        hooks[2]()
        send_groups(mirror_one, mirror, back, ss[1], rs[4:8], range(GROUPS // 2, GROUPS))

        def arrived(ref, g, sem):
            drain(ref[g].at[pl.ds(0, part - 2 if g == 0 else part)], sem)

        for g in range(GROUPS):
            arrived(came, g, rs[g])

            def forward(i4, total, g=g):
                for i in range(4):
                    i1 = i4 * 4 + i
                    j = g * part + i1
                    total = total * keep[0, j] + nt(came[g][index[2, j]], far[index[7, j]])
                    seg[i1] = total
                return total

            lax.fori_loop(0, part // 4, forward, zero)

            def add_forward(b, carry, g=g):
                near[:, block(b)] += seg[index[4, g * rb + b]] * keep[2, g * rb + b]
                return carry

            lax.fori_loop(0, rb, add_forward, 0)
        tail.wait_recv()
        near[:, 0 : bands * 128] += tails[turn]
        hooks[3]()
        for g in range(GROUPS):
            arrived(back, g, rs[4 + g])

            def backward(i4, total, g=g):
                for i in range(4):
                    i1 = i4 * 4 + i
                    j = g * part + i1
                    total = total * keep[1, j] + back[g][index[3, j]].astype(f32)
                    seg[i1] = total
                return total

            lax.fori_loop(0, part // 4, backward, zero)

            def add_backward(b, carry, g=g):
                total = near[:, block(b)] + seg[index[5, g * rb + b]] * keep[3, g * rb + b]
                if g < GROUPS - 1:
                    near[:, block(b)] = total
                else:
                    done(b, total)
                return carry

            lax.fori_loop(0, rb, add_backward, 0, unroll=4)
        halo.wait_send()
        tail.wait_send()
        drain(stage.at[pl.ds(0, slots - 2)], ss[0])
        drain(mirror.at[pl.ds(0, slots - 2)], ss[1])

    def first_done(b, total):
        d = root[pl.ds(b, 1), :]
        t = total * d
        t1[:, block(b)] = t
        u[b] = (t * d).astype(bf16)

    def last_done(b, total):
        t2[:, block(b)] = total * root[pl.ds(b, 1), :]

    apply(0, v, came1, back1, [lambda: None] * 4, first_done)
    saves.append(pltpu.make_async_copy(t1, t1_hbm, out_sem.at[1]))
    saves[1].start()

    kept = []
    lanes = functools.partial(jnp.concatenate, axis=1)

    def early_gram():
        (xh, xl), (ph, pl_) = halves(x0[...]), halves(t1[...])
        c11 = nt(ph, pl_)
        h01 = nt(xh, ph) + (nt(xh, pl_) + nt(xl, ph))
        mid_sum.start(lanes([h01, nt(ph, ph) + (c11 + c11.T)]))

    def early_step():
        sums = mid_sum.result() * (1.0 / points)
        h01, h11 = sums[:, :width], sums[:, width:]
        kept.extend((h00, h01, h11, *first_step(h00, h01, h11)))

    apply(1, u, came2, back2, [early_gram, mid_sum.across, mid_sum.gather, early_step], last_done)
    saves.append(pltpu.make_async_copy(t2, t2_hbm, out_sem.at[2]))
    saves[2].start()

    (th, tl), (xh, xl), (ph, pl_) = halves(t2[...]), halves(x0[...]), halves(t1[...])
    by_high = nt(jnp.concatenate([xh, ph, th], axis=0), th)
    low_by_high = nt(jnp.concatenate([xl, pl_, tl], axis=0), th)
    by_low = nt(jnp.concatenate([xh, ph], axis=0), tl)
    c22 = low_by_high[2 * width :]
    both = by_high[: 2 * width] + (by_low + low_by_high[: 2 * width])
    h02, h12 = both[:width], both[width:]
    h22 = by_high[2 * width :] + (c22 + c22.T)
    last_sum.start(jnp.concatenate([lanes([h02, h12]), lanes([h22, jnp.zeros_like(h22)])], axis=0))
    last_sum.across()
    last_sum.gather()
    sums = last_sum.result() * (1.0 / points)
    new, change = second_step(*kept, sums[:width, :width], sums[:width, width:], sums[width:, :width])
    coef[...] = jnp.zeros_like(coef)
    for i in range(3):
        coef[0:width, i * width : (i + 1) * width] = new[i]
        coef[width:, i * width : (i + 1) * width] = change[i]
    for save in saves:
        save.wait()
    deg_sent.wait_send()
    drain(cols.at[pl.ds(0, slots - 2)], small_sem.at[2])
    first_sum.close()
    mid_sum.close()
    last_sum.close()


def whole(n, tables, panel, diag_blocks, super_blocks, far_blocks):
    rb, bs = diag_blocks.shape[:2]
    bands, slots = super_blocks.shape[1], far_blocks.shape[0]
    width, owned = panel.shape
    index, keep = tables
    here = pl.BlockSpec(memory_space=pltpu.VMEM)
    away = pl.BlockSpec(memory_space=pl.ANY)
    scalar = pl.BlockSpec(memory_space=pltpu.SMEM)
    wide = jax.ShapeDtypeStruct((width, owned), f32)
    blocks = VMEM((slots, width, bs), bf16)
    return pl.pallas_call(
        functools.partial(whole_kernel, n, rb, bands, float(n * owned)),
        out_shape=(wide, wide, wide, jax.ShapeDtypeStruct((2 * width, 4 * width), f32)),
        in_specs=[scalar, scalar, here, away, away, away, away],
        out_specs=(away, away, away, here),
        scratch_shapes=[
            VMEM(diag_blocks.shape, bf16),
            VMEM(super_blocks.shape, bf16),
            VMEM(far_blocks.shape, bf16),
            VMEM((width, owned), f32),
            VMEM((width, owned), f32),
            VMEM((width, owned), f32),
            VMEM((rb, width, bs), bf16),
            VMEM((rb, width, bs), bf16),
            VMEM((rb, bs), f32),
            VMEM((2, bands, width, bs), bf16),
            VMEM((width, owned + bands * bs), f32),
            *[blocks] * 2,
            VMEM((slots // GROUPS, width, bs), f32),
            VMEM((2, width, bands * bs), f32),
            VMEM((rb + 8, bs), f32),
            VMEM((slots, bs), f32),
            VMEM((slots, 1, bs), f32),
            VMEM((slots, 1, bs), f32),
            VMEM((8, bs), f32),
            DMA((4,)),
            DMA((3,)),
            DMA((4,)),
            DMA((8,)),
            DMA((20,)),
            *[VMEM((slots // GROUPS, width, bs), bf16)] * (4 * GROUPS),
            *Reduction.scratch(width),
            *Reduction.scratch(width),
            *Reduction.scratch(2 * width),
        ],
        compiler_params=pltpu.CompilerParams(collective_id=1, has_side_effects=True, vmem_limit_bytes=VM_LIMIT),
        name="whole",
    )(index, keep, index, panel, diag_blocks, super_blocks, far_blocks)


def combine_kernel(coef, x0, t1, t2, basis, update):
    w = x0.shape[0]
    out = nn3(coef[:, 0 : 3 * w], jnp.concatenate([x0[...], t1[...], t2[...]], axis=0))
    basis[...] = out[:w]
    update[...] = out[w:]


def combine(coef, x0, t1, t2):
    w, owned = x0.shape
    chunk = 4096
    panel = pl.BlockSpec((w, chunk), lambda i: (0, i))
    return pl.pallas_call(
        combine_kernel,
        grid=(owned // chunk,),
        out_shape=(jax.ShapeDtypeStruct((w, owned), f32),) * 2,
        in_specs=[pl.BlockSpec(coef.shape, lambda i: (0, 0)), panel, panel, panel],
        out_specs=(panel, panel),
        compiler_params=pltpu.CompilerParams(vmem_limit_bytes=VM_LIMIT),
        name="combine",
    )(coef, x0, t1, t2)


def tables_kernel(n, rb, far_row, send_slot, index, keep):
    slots = far_row.shape[1]
    part = slots // GROUPS
    _, y, x, z, c = position()
    lane = lax.broadcasted_iota(i32, (1, slots), 1)
    other = lane // 2
    dz = (z - (other // 2) % 4 + 4) % 4
    group = (y - other // 32 - dz + 8) % 4
    place = (((x - (other // 8) % 4 - dz + 8) % 4) * 8 + dz * 2 + (c + other) % 2) * 2 + lane % 2
    rows, lanes = (lax.broadcasted_iota(i32, (slots, slots), d) for d in (0, 1))
    same = rows == lanes
    send, far = send_slot[...], far_row[...]
    index[...] = jnp.zeros_like(index)
    keep[...] = jnp.zeros_like(keep)
    index[0:1] = jnp.maximum(send, 0)
    index[1:2] = jnp.maximum(far, 0)
    index[6:7] = far
    index[8:9] = send
    places = jnp.sum(jnp.where(same, jnp.broadcast_to(place, same.shape), 0), axis=1, keepdims=True)
    stride = rb + 2
    target = (lane // rb) * stride + lane % rb + 1
    for at, key in ((0, far), (1, send)):
        kind = group * stride + key + 1
        mixed = kind * slots + lane
        column = jnp.sum(jnp.where(same, jnp.broadcast_to(mixed, same.shape), 0), axis=1, keepdims=True)
        rank = jnp.sum((mixed < column).astype(i32), axis=1, keepdims=True)
        hit = rank == lanes
        ranked = jnp.sum(jnp.where(hit, jnp.broadcast_to(column, hit.shape), 0), axis=0, keepdims=True)
        order = jnp.sum(jnp.where(hit, jnp.broadcast_to(places, hit.shape), 0), axis=0, keepdims=True)
        if at == 0:
            index[7:8] = ranked % slots
        ranked = ranked // slots
        before = jnp.concatenate([jnp.full((1, 1), -1, i32), ranked[:, :-1]], axis=1)
        kinds = column // slots
        last = jnp.sum((kinds <= target).astype(i32), axis=0, keepdims=True) - 1
        found = jnp.sum((kinds == target).astype(i32), axis=0, keepdims=True)
        index[2 + at : 3 + at] = order
        index[4 + at : 5 + at] = jnp.clip(last - (lane // rb) * part, 0, part - 1)
        keep[at : at + 1] = jnp.where(lane % part == 0, 0.0, (ranked == before).astype(f32))
        keep[2 + at : 3 + at] = (found > 0).astype(f32)


def tables_of(n, rb, far_row, send_slot):
    slots = far_row.shape[0]
    here = pl.BlockSpec(memory_space=pltpu.VMEM)
    return pl.pallas_call(
        functools.partial(tables_kernel, n, rb),
        out_shape=(
            jax.ShapeDtypeStruct((16, slots), i32),
            jax.ShapeDtypeStruct((8, slots), f32),
        ),
        in_specs=[here, here],
        out_specs=(here, here),
        name="tables",
    )(far_row.reshape(1, slots), send_slot.reshape(1, slots))


def shards(diag_blocks, super_blocks, far_blocks, far_row, send_slot, panel):
    n = lax.axis_size("curve")
    tables = tables_of(n, diag_blocks.shape[0], far_row, send_slot)
    x0, t1, t2, coef = whole(n, tables, panel, diag_blocks, super_blocks, far_blocks)
    return combine(coef, x0, t1, t2)


def solution(mesh):
    return jax.shard_map(
        shards,
        mesh=mesh,
        in_specs=(
            P("curve", None, None),
            P("curve", None, None, None),
            P("curve", None, None),
            P("curve"),
            P("curve"),
            P(None, "curve"),
        ),
        out_specs=(P(None, "curve"), P(None, "curve")),
        check_vma=False,
    )
```
